32 devices in a mesh: band: 4 (over x, core), gvec: 2 (over y), dom: 4 (over z).
Axes of the slice: x: 2, y: 2, z: 4, core: 2. Of those that a mesh axis runs over, the one named last changes fastest.
Arguments:
- coeffs: bfloat16 [16, 128, 128, 128], P(('band', 'dom'), 'gvec'), may hold values from -1.5 to 1.5
- v_local: bfloat16 [128, 128, 128], P(None, 'gvec'), may hold values from -4 to 4
- atom_pos: float32 [3, 32768], P(None, ('band', 'gvec', 'dom')), may hold values from -32 to 160
- atom_charge: float32 [32768], P(('band', 'gvec', 'dom')), may hold values from -1 to 1
- near_list: int32 [512], P(('band', 'gvec', 'dom')), may hold values from 0 to 1023, as said below
- live_count: int32 [32], P(('band', 'gvec', 'dom')), may hold values from 0 to 16, as said below
Outputs:
- waves_new: bfloat16 [16, 128, 128, 128], P(('band', 'dom'), 'gvec')
- energies: float32 [16], P(('band', 'dom'))
- resid_ratio: float32 [16], P(('band', 'dom'))
- atom_force: float32 [3, 32768], P(None, ('band', 'gvec', 'dom'))
- totals: float32 [8], replicated
The draws below stay inside these ranges and needn't reach their ends.
Inputs may be any that keep to these rules, and one draw needn't show every extreme that they name: `live_count`: the counts of all devices sum to exactly 128; some device has all 16 slots live; a device's live slots are its first ones. `near_list`: indices of the device's own atoms; the 16 entries of one device's block are distinct.
All inputs are finite; a program needn't handle non-finite values.
Results may differ from the reference program's by a relative error of at most 0.0045.
Values may be sent and summed in bfloat16 or wider, within the bound.
A program may use at most 64 MiB of HBM per device.

```python
import jax
import jax.numpy as jnp
from jax import lax

GRID = 128
CAP = 16
ATOMS_DEV = 1024
BANDS = 16
NCH = 512
LIVE = 128
NATOMS = 32768


def draw_live_count(key, part):
    owners = NCH // CAP
    key_level, key_leader, key_order = jax.random.split(key, 3)
    levels = jax.random.randint(key_level, (owners,), 0, 3)
    leader = jax.random.randint(key_leader, (), 0, owners)
    levels = jnp.where(jnp.arange(owners) == leader, 3, levels)
    shuffle = jax.random.permutation(key_order, NCH)
    scores = jnp.repeat(levels, CAP) * NCH + shuffle
    _, chosen = lax.top_k(scores, LIVE)
    counts = jnp.zeros((owners,), jnp.int32).at[chosen // CAP].add(1)
    return counts.astype(jnp.int32)


def draw_near_list(key, part):
    owners = NCH // CAP
    key_lists = jax.random.split(key, owners)

    def pick_atoms(key_one):
        return jax.random.permutation(key_one, ATOMS_DEV)[:CAP]
    lists = jax.vmap(pick_atoms)(key_lists)
    return lists.reshape(-1).astype(jnp.int32)


def block_scale(key, dims, cuts, least, high):
    level, own = 1.0, jax.random.fold_in(key, 6)
    for axis_at, shards_of in cuts:
        draws = jnp.exp(jax.random.uniform(jax.random.fold_in(own, axis_at), (shards_of,), jnp.float32, least / len(cuts), high / len(cuts)))
        level = level * jnp.repeat(draws, dims[axis_at] // shards_of).reshape([-1 if axis == axis_at else 1 for axis in range(len(dims))])
    return level


def scatter_about(key, shape, spread, most, cuts=(), kind=jnp.bfloat16):
    result = jax.random.normal(key, shape, jnp.float32) * spread
    if len(cuts) > 0:
        result = block_scale(key, shape, cuts, -0.22, 0.18) * result
    return jnp.clip(result, min=-most, max=most).astype(kind)


def setup_inputs(seed: int = 0) -> dict:
    splits = jax.random.split(jax.random.key(seed), 7)
    return {
        "coeffs": scatter_about(splits[0], (BANDS, GRID, GRID, GRID), 0.25, 1.5, ((0, 16), (1, 2))),
        "v_local": scatter_about(splits[1], (GRID, GRID, GRID), 1.0, 4.0, ((1, 2),)),
        "atom_pos": jnp.clip(-32.0 + 192.0 * jax.random.uniform(splits[2], (3, NATOMS), jnp.float32) ** block_scale(splits[2], (3, NATOMS), ((1, 32),), -0.2, 0.2), -32.0, 160.0),
        "atom_charge": jnp.clip(jax.random.uniform(splits[3], (NATOMS,), jnp.float32, -1.0, 1.0) * block_scale(splits[3], (NATOMS,), ((0, 32),), -0.4, 0.0), -1.0, 1.0),
        "near_list": draw_near_list(jax.random.fold_in(splits[6], 71), 0),
        "live_count": draw_live_count(jax.random.fold_in(splits[6], 71), 0),
    }


sigma_fractions = (1.0 / 32.0, 1.0 / 16.0, 1.0 / 8.0, 1.0 / 4.0)
kernel_weights = (1.0, 0.5, 0.25, 0.125)
force_unit = 1.0 / 4096.0
step_size = 0.5

def cosine_table(length):
    points = jnp.arange(length).astype(jnp.float32)
    angles = jnp.pi * (points[:, None] + 0.5) * points[None, :] / length
    scales = jnp.where(points == 0.0, jnp.sqrt(1.0 / length), jnp.sqrt(2.0 / length))
    return (jnp.cos(angles) * scales[None, :]).astype(jnp.bfloat16)

def occupancy(band_index, band_total):
    shifted = band_index.astype(jnp.float32) - 0.5 * band_total
    return 2.0 / (1.0 + jnp.exp(shifted / (0.125 * band_total)))

def kernels(points, centres, extent):
    values = []
    slopes = []
    for fraction in sigma_fractions:
        exponent = 0.5 / (extent * fraction) ** 2
        offset = points[:, None] - centres[None, :]
        gauss_value = jnp.exp(-exponent * offset * offset)
        values.append(gauss_value)
        slopes.append(2.0 * exponent * offset * gauss_value)
    return (jnp.concatenate(values, axis=1), jnp.concatenate(slopes, axis=1))

def charge_work(charges, density, x_start, y_start, extent, block_width):
    x_count, y_count, z_count = density.shape
    density_rows = density.reshape(x_count * y_count, z_count).astype(jnp.bfloat16)
    x_points = (x_start + jnp.arange(x_count)).astype(jnp.float32)
    y_points = (y_start + jnp.arange(y_count)).astype(jnp.float32)
    z_points = jnp.arange(z_count).astype(jnp.float32)
    weights = jnp.array(kernel_weights, jnp.float32)
    slot_total = charges.shape[1]
    blocks = charges.reshape(4, slot_total // block_width, block_width).transpose(1, 0, 2)

    def one_block(potential, block_now):
        x_value, x_slope = kernels(x_points, block_now[0], extent)
        y_value, y_slope = kernels(y_points, block_now[1], extent)
        z_value, z_slope = kernels(z_points, block_now[2], extent)
        scaled = (weights[:, None] * block_now[3][None, :]).reshape(-1)
        plane = (x_value[:, None, :] * y_value[None, :, :]).reshape(x_count * y_count, -1).astype(jnp.bfloat16)
        depth = (scaled[None, :] * z_value).astype(jnp.bfloat16)
        potential = potential + lax.dot_general(plane, depth, (((1,), (1,)), ((), ())), preferred_element_type=jnp.float32)
        tables = jnp.concatenate([z_value, z_slope], axis=1).astype(jnp.bfloat16)
        projected = jnp.dot(density_rows, tables, preferred_element_type=jnp.float32).reshape(x_count, y_count, 2, -1)
        grid_part = projected[:, :, 0, :]
        slope_part = projected[:, :, 1, :]
        along_y = lax.optimization_barrier(jnp.sum(grid_part * y_value[None], axis=1))
        slope_y = lax.optimization_barrier(jnp.sum(grid_part * y_slope[None], axis=1))
        depth_y = lax.optimization_barrier(jnp.sum(slope_part * y_value[None], axis=1))
        force_x = lax.optimization_barrier(jnp.sum(x_slope * along_y, axis=0))
        force_y = lax.optimization_barrier(jnp.sum(x_value * slope_y, axis=0))
        force_z = lax.optimization_barrier(jnp.sum(x_value * depth_y, axis=0))
        stacked = jnp.stack([force_x, force_y, force_z]) * scaled[None, :]
        forces = -force_unit * lax.optimization_barrier(jnp.sum(stacked.reshape(3, len(kernel_weights), -1), axis=1))
        return (potential, forces)
    start = jnp.zeros((x_count * y_count, z_count), jnp.float32)
    potential, forces = lax.scan(one_block, start, blocks)
    return (potential.reshape(x_count, y_count, z_count), forces.transpose(1, 0, 2).reshape(3, slot_total))

def stress_terms(weighted, x_wave, y_wave):
    over_z = lax.optimization_barrier(jnp.sum(weighted, axis=2))
    over_y = lax.optimization_barrier(jnp.sum(weighted, axis=1))
    over_x = lax.optimization_barrier(jnp.sum(weighted, axis=0))
    stress_xx = jnp.sum(x_wave * x_wave * lax.optimization_barrier(jnp.sum(over_z, axis=1)))
    stress_yy = jnp.sum(y_wave * y_wave * lax.optimization_barrier(jnp.sum(over_z, axis=0)))
    stress_zz = jnp.sum(y_wave * y_wave * lax.optimization_barrier(jnp.sum(over_y, axis=0)))
    stress_xy = jnp.sum(x_wave[:, None] * y_wave[None, :] * over_z)
    stress_xz = jnp.sum(x_wave[:, None] * y_wave[None, :] * over_y)
    stress_yz = jnp.sum(y_wave[:, None] * y_wave[None, :] * over_x)
    return jnp.stack([stress_xx, stress_yy, stress_zz, stress_xy, stress_xz, stress_yz])

def forward_band(coeff_band, cosine_wide):
    sectioned = jnp.einsum('aql,zl->aqz', coeff_band.astype(jnp.float32), cosine_wide).astype(jnp.bfloat16)
    sectioned = jnp.einsum('aqz,yq->ayz', sectioned.astype(jnp.float32), cosine_wide).astype(jnp.bfloat16)
    return jnp.einsum('ayz,xa->xyz', sectioned.astype(jnp.float32), cosine_wide).astype(jnp.bfloat16)

def backward_band(applied, cosine_wide):
    sectioned = jnp.einsum('xyz,xa->ayz', applied.astype(jnp.float32), cosine_wide).astype(jnp.bfloat16)
    sectioned = jnp.einsum('ayz,yq->aqz', sectioned.astype(jnp.float32), cosine_wide).astype(jnp.bfloat16)
    return jnp.einsum('aqz,zl->aql', sectioned.astype(jnp.float32), cosine_wide)

def reference(coeffs, v_local, atom_pos, atom_charge, near_list, live_count):
    cosines = cosine_table(GRID)
    cosine_wide = cosines.astype(jnp.float32)
    occupied = occupancy(jnp.arange(BANDS), BANDS)

    def add_band(density, inputs):
        coeff_band, weight = inputs
        real_space = forward_band(coeff_band, cosine_wide).astype(jnp.float32)
        return (density + weight * real_space * real_space, None)
    density, _ = lax.scan(add_band, jnp.zeros((GRID, GRID, GRID), jnp.float32), (coeffs, occupied))
    owners = jnp.arange(NCH) // CAP
    slot_index = jnp.arange(NCH) % CAP
    live_mask = (slot_index < live_count[owners]).astype(jnp.float32)
    atom_index = (owners * ATOMS_DEV + near_list).astype(jnp.int32)
    picked = jnp.concatenate([atom_pos[:, atom_index], (atom_charge[atom_index] * live_mask)[None, :]], axis=0)
    target = jnp.where(live_mask > 0.5, jnp.cumsum(live_mask) - 1.0, 1.0 * LIVE).astype(jnp.int32)
    charges = jnp.zeros((4, LIVE), jnp.float32).at[:, target].set(picked, mode='drop')
    potential, forces = charge_work(charges, density, 0, 0, GRID, min(256, LIVE))
    padded = forces[:, jnp.minimum(target, LIVE - 1)] * live_mask[None, :]
    atom_force = jnp.zeros((3, NATOMS), jnp.float32).at[:, atom_index].add(padded)
    embedding = jnp.sum(density * potential) / GRID ** 3
    rounded = lax.optimization_barrier(potential.astype(jnp.bfloat16))
    field_total = v_local.astype(jnp.float32) + rounded.astype(jnp.float32)
    wave_index = jnp.arange(GRID).astype(jnp.float32) * (jnp.pi / GRID)
    kinetic = 0.5 * (wave_index[:, None, None] ** 2 + wave_index[None, :, None] ** 2 + wave_index[None, None, :] ** 2)

    def update_band(weighted, inputs):
        coeff_band, weight = inputs
        real_space = forward_band(coeff_band, cosine_wide)
        applied = (field_total * real_space.astype(jnp.float32)).astype(jnp.bfloat16)
        wave_field = backward_band(applied, cosine_wide)
        coeff_wide = coeff_band.astype(jnp.float32)
        image = kinetic * coeff_wide + wave_field
        norm_sq = jnp.sum(coeff_wide * coeff_wide)
        energy = jnp.sum(coeff_wide * image) / norm_sq
        residual = image - energy * coeff_wide
        ratio_band = jnp.sum(residual * residual) / norm_sq
        updated = (coeff_wide - step_size * residual / (1.0 + kinetic)).astype(jnp.bfloat16)
        return (weighted + weight * coeff_wide * coeff_wide, (updated, energy, ratio_band))
    weighted, outputs = lax.scan(update_band, jnp.zeros((GRID, GRID, GRID), jnp.float32), (coeffs, occupied))
    waves_new, energies, resid_ratio = outputs
    stress = stress_terms(weighted, wave_index, wave_index) / GRID ** 3
    band_energy = jnp.sum(occupied * energies) / BANDS
    totals = jnp.concatenate([stress, jnp.stack([embedding, band_energy])])
    return (waves_new, energies, resid_ratio, atom_force, totals)
```

```python
import jax
import jax.numpy as jnp
from jax import lax
from jax.experimental import pallas as pl
from jax.experimental.pallas import tpu as pltpu
from jax.sharding import PartitionSpec as P
import functools

sigma_fractions = (1.0 / 32.0, 1.0 / 16.0, 1.0 / 8.0, 1.0 / 4.0)
kernel_weights = (1.0, 0.5, 0.25, 0.125)
force_unit = 1.0 / 4096.0
step_size = 0.5


def cosine_table(length):
    points = jnp.arange(length).astype(jnp.float32)
    angles = jnp.pi * (points[:, None] + 0.5) * points[None, :] / length
    scales = jnp.where(points == 0.0, jnp.sqrt(1.0 / length), jnp.sqrt(2.0 / length))
    return (jnp.cos(angles) * scales[None, :]).astype(jnp.bfloat16)


def occupancy(band_index, band_total):
    shifted = band_index.astype(jnp.float32) - 0.5 * band_total
    return 2.0 / (1.0 + jnp.exp(shifted / (0.125 * band_total)))


def kernels(points, centres, extent):
    values = []
    slopes = []
    for fraction in sigma_fractions:
        exponent = 0.5 / (extent * fraction) ** 2
        offset = points[:, None] - centres[None, :]
        gauss_value = jnp.exp(-exponent * offset * offset)
        values.append(gauss_value)
        slopes.append(2.0 * exponent * offset * gauss_value)
    return (jnp.concatenate(values, axis=1), jnp.concatenate(slopes, axis=1))


def stress_terms(weighted, x_wave, y_wave):
    over_z = jnp.sum(weighted, axis=2)
    over_y = jnp.sum(weighted, axis=1)
    over_x = jnp.sum(weighted, axis=0)
    stress_xx = jnp.sum(x_wave * x_wave * jnp.sum(over_z, axis=1))
    stress_yy = jnp.sum(y_wave * y_wave * jnp.sum(over_z, axis=0))
    stress_zz = jnp.sum(y_wave * y_wave * jnp.sum(over_y, axis=0))
    stress_xy = jnp.sum(x_wave[:, None] * y_wave[None, :] * over_z)
    stress_xz = jnp.sum(x_wave[:, None] * y_wave[None, :] * over_y)
    stress_yz = jnp.sum(y_wave[:, None] * y_wave[None, :] * over_x)
    return jnp.stack([stress_xx, stress_yy, stress_zz, stress_xy, stress_xz, stress_yz])


def peer_coords(index, sizes):
    _, gvec_size, dom_size = sizes
    return (index // (gvec_size * dom_size), (index // dom_size) % gvec_size, index % dom_size)


def gather_kernel(sizes, x_ref, out_ref, send_sem, recv_sem):
    total = sizes[0] * sizes[1] * sizes[2]
    me = (lax.axis_index("band") * sizes[1] + lax.axis_index("gvec")) * sizes[2] + lax.axis_index("dom")
    barrier = pltpu.get_barrier_semaphore()

    def greet(step, carry):
        peer = lax.rem(me + step, total)
        pl.semaphore_signal(
            barrier, inc=1, device_id=peer_coords(peer, sizes), device_id_type=pl.DeviceIdType.MESH
        )
        return carry

    def copy_of(step):
        peer = lax.rem(me + step, total)
        return pltpu.make_async_remote_copy(
            src_ref=x_ref,
            dst_ref=out_ref.at[me],
            send_sem=send_sem.at[step],
            recv_sem=recv_sem.at[step],
            device_id=peer_coords(peer, sizes),
            device_id_type=pl.DeviceIdType.MESH,
        )

    def send(step, carry):
        copy_of(step).start()
        return carry

    def finish(step, carry):
        copy_of(step).wait()
        return carry

    lax.fori_loop(1, total, greet, 0)
    out_ref[me] = x_ref[...]
    pl.semaphore_wait(barrier, total - 1)
    lax.fori_loop(1, total, send, 0)
    lax.fori_loop(1, total, finish, 0)


def gather_all(block, sizes, collective_id):
    total = sizes[0] * sizes[1] * sizes[2]
    return pl.pallas_call(
        functools.partial(gather_kernel, sizes),
        out_shape=jax.ShapeDtypeStruct((total,) + block.shape, block.dtype),
        in_specs=[pl.BlockSpec(memory_space=pltpu.VMEM)],
        out_specs=pl.BlockSpec(memory_space=pltpu.VMEM),
        scratch_shapes=[pltpu.SemaphoreType.DMA((total,)), pltpu.SemaphoreType.DMA((total,))],
        compiler_params=pltpu.CompilerParams(collective_id=collective_id, has_side_effects=True),
        name=f"gather_{collective_id}",
    )(block)


def pair_kernel(gvec_size, x_ref, out_ref, send_sem, recv_sem):
    me = lax.axis_index("gvec")
    barrier = pltpu.get_barrier_semaphore()
    others = [lax.rem(me + step, gvec_size) for step in range(1, gvec_size)]
    band, dom = lax.axis_index("band"), lax.axis_index("dom")
    for peer in others:
        pl.semaphore_signal(
            barrier, inc=1, device_id=(band, peer, dom), device_id_type=pl.DeviceIdType.MESH
        )
    out_ref[me] = x_ref[...]
    pl.semaphore_wait(barrier, gvec_size - 1)
    copies = []
    for step, peer in enumerate(others):
        copy = pltpu.make_async_remote_copy(
            src_ref=x_ref,
            dst_ref=out_ref.at[me],
            send_sem=send_sem.at[step],
            recv_sem=recv_sem.at[step],
            device_id=(band, peer, dom),
            device_id_type=pl.DeviceIdType.MESH,
        )
        copy.start()
        copies.append(copy)
    for copy in copies:
        copy.wait()


def gather_gvec(block, gvec_size, collective_id):
    return pl.pallas_call(
        functools.partial(pair_kernel, gvec_size),
        out_shape=jax.ShapeDtypeStruct((gvec_size,) + block.shape, block.dtype),
        in_specs=[pl.BlockSpec(memory_space=pltpu.VMEM)],
        out_specs=pl.BlockSpec(memory_space=pltpu.VMEM),
        scratch_shapes=[pltpu.SemaphoreType.DMA((gvec_size,)), pltpu.SemaphoreType.DMA((gvec_size,))],
        compiler_params=pltpu.CompilerParams(collective_id=collective_id, has_side_effects=True),
        name=f"gather_{collective_id}",
    )(block)


def potential_kernel(x_ref, y_ref, depth_ref, local_ref, out_ref):
    rows = x_ref.shape[0]
    for row in range(rows):
        plane = (x_ref[row : row + 1, :] * y_ref[...]).astype(jnp.bfloat16)
        value = lax.dot_general(
            plane, depth_ref[...], (((1,), (1,)), ((), ())), preferred_element_type=jnp.float32
        )
        rounded = value.astype(jnp.bfloat16).astype(jnp.float32)
        out_ref[row] = local_ref[row].astype(jnp.float32) + rounded


def slab_potential(x_value, y_value, depth, v_local):
    x_total, y_total, z_total = v_local.shape
    width = x_value.shape[1]
    rows = 8
    return pl.pallas_call(
        potential_kernel,
        grid=(x_total // rows,),
        out_shape=jax.ShapeDtypeStruct(v_local.shape, jnp.float32),
        in_specs=[
            pl.BlockSpec((rows, width), lambda i: (i, 0)),
            pl.BlockSpec((y_total, width), lambda i: (0, 0)),
            pl.BlockSpec((z_total, width), lambda i: (0, 0)),
            pl.BlockSpec((rows, y_total, z_total), lambda i: (i, 0, 0)),
        ],
        out_specs=pl.BlockSpec((rows, y_total, z_total), lambda i: (i, 0, 0)),
        cost_estimate=pl.CostEstimate(
            flops=2 * x_total * y_total * z_total * width,
            bytes_accessed=6 * x_total * y_total * z_total,
            transcendentals=0,
        ),
        name="slab_potential",
    )(x_value, y_value, depth, v_local)


def force_kernel(xv_ref, xs_ref, yv_ref, ys_ref, density_ref, out_ref):
    @pl.when(pl.program_id(0) == 0)
    def _():
        out_ref[...] = jnp.zeros_like(out_ref)

    rows, y_total, z_total = density_ref.shape
    width = yv_ref.shape[1]
    density = density_ref[...].astype(jnp.float32)
    density = (density * density).astype(jnp.bfloat16).reshape(rows * y_total, z_total)
    for part, (xr, yr) in enumerate(((xv_ref, yv_ref), (xs_ref, yv_ref), (xv_ref, ys_ref))):
        plane = jnp.concatenate(
            [(xr[row : row + 1, :] * yr[...]).astype(jnp.bfloat16) for row in range(rows)], axis=0
        )
        out_ref[part] += lax.dot_general(
            density, plane, (((0,), (0,)), ((), ())), preferred_element_type=jnp.float32
        )


def slab_moments(x_value, x_slope, y_value, y_slope, real_space):
    x_total, y_total, z_total = real_space.shape
    width = x_value.shape[1]
    rows = 8
    return pl.pallas_call(
        force_kernel,
        grid=(x_total // rows,),
        out_shape=jax.ShapeDtypeStruct((3, z_total, width), jnp.float32),
        in_specs=[
            pl.BlockSpec((rows, width), lambda i: (i, 0)),
            pl.BlockSpec((rows, width), lambda i: (i, 0)),
            pl.BlockSpec((y_total, width), lambda i: (0, 0)),
            pl.BlockSpec((y_total, width), lambda i: (0, 0)),
            pl.BlockSpec((rows, y_total, z_total), lambda i: (i, 0, 0)),
        ],
        out_specs=pl.BlockSpec((3, z_total, width), lambda i: (0, 0, 0)),
        cost_estimate=pl.CostEstimate(
            flops=6 * x_total * y_total * z_total * width,
            bytes_accessed=2 * x_total * y_total * z_total,
            transcendentals=0,
        ),
        name="slab_moments",
    )(x_value, x_slope, y_value, y_slope, real_space)


def per_device(sizes, coeffs, v_local, atom_pos, atom_charge, near_list, live_count):
    local_bands, x_local, extent, _ = coeffs.shape
    cosines = cosine_table(extent)
    gvec_id = lax.axis_index("gvec")
    group_id = lax.axis_index("band") * sizes[2] + lax.axis_index("dom")
    me = (lax.axis_index("band") * sizes[1] + gvec_id) * sizes[2] + lax.axis_index("dom")
    groups = sizes[0] * sizes[2]
    devices = groups * sizes[1]
    band_total = local_bands * groups
    cell_count = float(extent**3)
    band_ids = group_id * local_bands + jnp.arange(local_bands)
    weight = occupancy(band_ids, band_total)
    capacity = near_list.shape[0]
    live_mask = (jnp.arange(capacity) < live_count[0]).astype(jnp.float32)
    picked_pos = jnp.take(atom_pos, near_list, axis=1)
    picked_charge = jnp.take(atom_charge, near_list) * live_mask
    own_block = jnp.concatenate([picked_pos, picked_charge[None, :], live_mask[None, :]], axis=0)
    lanes = -(-capacity // 128) * 128
    tile = jnp.pad(own_block, ((0, 3), (0, lanes - capacity)))
    gathered = gather_all(tile, sizes, 0)
    all_blocks = gathered[:, :5, :capacity].transpose(1, 0, 2).reshape(5, devices * capacity)
    live_total = all_blocks.shape[1] // 4
    order = jnp.cumsum(all_blocks[4]) - 1.0
    target = jnp.where(all_blocks[4] > 0.5, order, float(live_total)).astype(jnp.int32)
    select = (target[:, None] == jnp.arange(live_total)[None, :]).astype(jnp.float32)
    charges = jnp.dot(all_blocks[:4], select, precision=lax.Precision.HIGHEST)

    y_share = v_local.shape[1]
    x_points = jnp.arange(extent).astype(jnp.float32)
    y_points = (gvec_id * y_share + jnp.arange(y_share)).astype(jnp.float32)
    x_value, x_slope = kernels(x_points, charges[0], extent)
    y_value, y_slope = kernels(y_points, charges[1], extent)
    z_value, z_slope = kernels(x_points, charges[2], extent)
    weights = jnp.array(kernel_weights, jnp.float32)
    scaled = (weights[:, None] * charges[3][None, :]).reshape(-1)
    depth = (scaled[None, :] * z_value).astype(jnp.bfloat16)
    field_total = slab_potential(x_value, y_value, depth, v_local)

    sectioned = jnp.einsum(
        "naql,zl->naqz", coeffs, cosines, preferred_element_type=jnp.float32
    ).astype(jnp.bfloat16)
    sectioned = jnp.einsum(
        "naqz,yq->nayz", sectioned, cosines, preferred_element_type=jnp.float32
    ).astype(jnp.bfloat16)
    exchanged = lax.all_to_all(sectioned, "gvec", split_axis=2, concat_axis=1, tiled=True)
    real_space = jnp.einsum(
        "nayz,xa->nxyz", exchanged, cosines, preferred_element_type=jnp.float32
    ).astype(jnp.bfloat16)
    applied = (field_total[None] * real_space.astype(jnp.float32)).astype(jnp.bfloat16)
    moments = 0.0
    for band in range(local_bands):
        moments = moments + weight[band] * slab_moments(
            x_value, x_slope, y_value, y_slope, real_space[band]
        )
    embedding = jnp.sum(moments[0] * depth.astype(jnp.float32)) / cell_count
    force_terms = jnp.stack(
        [
            jnp.sum(moments[1] * z_value, axis=0),
            jnp.sum(moments[2] * z_value, axis=0),
            jnp.sum(moments[0] * z_slope, axis=0),
        ]
    )
    force_terms = force_terms * scaled[None, :]
    forces = -force_unit * jnp.sum(force_terms.reshape(3, len(kernel_weights), -1), axis=1)

    back_one = jnp.einsum(
        "nxyz,xa->nayz", applied, cosines, preferred_element_type=jnp.float32
    ).astype(jnp.bfloat16)
    returned = lax.all_to_all(back_one, "gvec", split_axis=1, concat_axis=2, tiled=True)
    back_two = jnp.einsum(
        "nayz,yq->naqz", returned, cosines, preferred_element_type=jnp.float32
    ).astype(jnp.bfloat16)
    wave_field = jnp.einsum("naqz,zl->naql", back_two, cosines, preferred_element_type=jnp.float32)
    wave_step = jnp.pi / extent
    x_wave = (gvec_id * x_local + jnp.arange(x_local)).astype(jnp.float32) * wave_step
    y_wave = jnp.arange(extent).astype(jnp.float32) * wave_step
    kinetic = 0.5 * (
        x_wave[:, None, None] ** 2 + y_wave[None, :, None] ** 2 + y_wave[None, None, :] ** 2
    )
    coeff_wide = coeffs.astype(jnp.float32)
    image = kinetic[None] * coeff_wide + wave_field
    norm_part = jnp.sum(coeff_wide * coeff_wide, axis=(1, 2, 3))
    inner_part = jnp.sum(coeff_wide * image, axis=(1, 2, 3))
    pair_block = jnp.pad(
        jnp.stack([norm_part, inner_part]), ((0, 6), (0, -local_bands % 128))
    )
    pair = jnp.sum(gather_gvec(pair_block, sizes[1], 1), axis=0)
    norm_sq = pair[0, :local_bands]
    energies = pair[1, :local_bands] / norm_sq
    residual = image - energies[:, None, None, None] * coeff_wide
    resid_part = jnp.sum(residual * residual, axis=(1, 2, 3))
    waves_new = (coeff_wide - step_size * residual / (1.0 + kinetic[None])).astype(jnp.bfloat16)
    weighted = jnp.sum(weight[:, None, None, None] * coeff_wide * coeff_wide, axis=0)
    stress_local = stress_terms(weighted, x_wave, y_wave) / cell_count
    band_part = jnp.sum(weight * inner_part / norm_sq) / band_total
    local_totals = jnp.concatenate([stress_local, embedding[None], band_part[None]])
    mine = (jnp.arange(band_total)[None, :] == band_ids[:, None]).astype(jnp.float32)
    resid_vec = jnp.sum(mine * resid_part[:, None], axis=0)
    flat = jnp.concatenate([forces.reshape(-1), local_totals, resid_vec])
    flat = jnp.pad(flat, (0, -flat.shape[0] % 1024)).reshape(-1, 128)
    summed = jnp.sum(gather_all(flat, sizes, 2), axis=0).reshape(-1)
    force_all = summed[: 3 * live_total].reshape(3, live_total)
    totals = summed[3 * live_total : 3 * live_total + 8]
    resid_all = summed[3 * live_total + 8 : 3 * live_total + 8 + band_total]
    resid_ratio = jnp.sum(mine * resid_all[None, :], axis=1) / norm_sq
    start = lax.dynamic_slice(order, (me * capacity,), (capacity,))
    own_target = jnp.where(live_mask > 0.5, start, float(live_total)).astype(jnp.int32)
    slot_select = (own_target[None, :] == jnp.arange(live_total)[:, None]).astype(jnp.float32)
    slot_force = jnp.dot(force_all, slot_select, precision=lax.Precision.HIGHEST)
    atom_select = (near_list[:, None] == jnp.arange(atom_pos.shape[1])[None, :]).astype(jnp.float32)
    atom_force = jnp.dot(slot_force, atom_select, precision=lax.Precision.HIGHEST)
    return (waves_new, energies, resid_ratio, atom_force, totals)


def solution(mesh):
    sizes = (mesh.shape["band"], mesh.shape["gvec"], mesh.shape["dom"])
    return jax.shard_map(
        functools.partial(per_device, sizes),
        mesh=mesh,
        in_specs=(
            P(("band", "dom"), "gvec", None, None),
            P(None, "gvec", None),
            P(None, ("band", "gvec", "dom")),
            P(("band", "gvec", "dom")),
            P(("band", "gvec", "dom")),
            P(("band", "gvec", "dom")),
        ),
        out_specs=(
            P(("band", "dom"), "gvec", None, None),
            P(("band", "dom")),
            P(("band", "dom")),
            P(None, ("band", "gvec", "dom")),
            P(),
        ),
        check_vma=False,
    )
```

```python
import jax
import jax.numpy as jnp
from jax import lax
from jax.experimental import pallas as pl
from jax.experimental.pallas import tpu as pltpu
from jax.sharding import PartitionSpec as P
import functools

sigma_fractions = (1.0 / 32.0, 1.0 / 16.0, 1.0 / 8.0, 1.0 / 4.0)
kernel_weights = (1.0, 0.5, 0.25, 0.125)
force_unit = 1.0 / 4096.0
step_size = 0.5


def cosine_table(length):
    points = jnp.arange(length).astype(jnp.float32)
    angles = jnp.pi * (points[:, None] + 0.5) * points[None, :] / length
    scales = jnp.where(points == 0.0, jnp.sqrt(1.0 / length), jnp.sqrt(2.0 / length))
    return (jnp.cos(angles) * scales[None, :]).astype(jnp.bfloat16)


def occupancy(band_index, band_total):
    shifted = band_index.astype(jnp.float32) - 0.5 * band_total
    return 2.0 / (1.0 + jnp.exp(shifted / (0.125 * band_total)))


def kernels(points, centres, extent):
    values = []
    slopes = []
    for fraction in sigma_fractions:
        exponent = 0.5 / (extent * fraction) ** 2
        offset = points[:, None] - centres[None, :]
        gauss_value = jnp.exp(-exponent * offset * offset)
        values.append(gauss_value)
        slopes.append(2.0 * exponent * offset * gauss_value)
    return (jnp.concatenate(values, axis=1), jnp.concatenate(slopes, axis=1))


def stress_terms(weighted, x_wave, y_wave):
    over_z = jnp.sum(weighted, axis=2)
    over_y = jnp.sum(weighted, axis=1)
    over_x = jnp.sum(weighted, axis=0)
    stress_xx = jnp.sum(x_wave * x_wave * jnp.sum(over_z, axis=1))
    stress_yy = jnp.sum(y_wave * y_wave * jnp.sum(over_z, axis=0))
    stress_zz = jnp.sum(y_wave * y_wave * jnp.sum(over_y, axis=0))
    stress_xy = jnp.sum(x_wave[:, None] * y_wave[None, :] * over_z)
    stress_xz = jnp.sum(x_wave[:, None] * y_wave[None, :] * over_y)
    stress_yz = jnp.sum(y_wave[:, None] * y_wave[None, :] * over_x)
    return jnp.stack([stress_xx, stress_yy, stress_zz, stress_xy, stress_xz, stress_yz])


def peer_coords(index, sizes):
    _, gvec_size, dom_size = sizes
    return (index // (gvec_size * dom_size), (index // dom_size) % gvec_size, index % dom_size)


def gather_kernel(sizes, x_ref, out_ref, send_sem, recv_sem):
    total = sizes[0] * sizes[1] * sizes[2]
    me = (lax.axis_index("band") * sizes[1] + lax.axis_index("gvec")) * sizes[2] + lax.axis_index("dom")
    barrier = pltpu.get_barrier_semaphore()

    def greet(step, carry):
        peer = lax.rem(me + step, total)
        pl.semaphore_signal(
            barrier, inc=1, device_id=peer_coords(peer, sizes), device_id_type=pl.DeviceIdType.MESH
        )
        return carry

    def copy_of(step):
        peer = lax.rem(me + step, total)
        return pltpu.make_async_remote_copy(
            src_ref=x_ref,
            dst_ref=out_ref.at[me],
            send_sem=send_sem.at[step],
            recv_sem=recv_sem.at[step],
            device_id=peer_coords(peer, sizes),
            device_id_type=pl.DeviceIdType.MESH,
        )

    def send(step, carry):
        copy_of(step).start()
        return carry

    def finish(step, carry):
        copy_of(step).wait()
        return carry

    lax.fori_loop(1, total, greet, 0)
    out_ref[me] = x_ref[...]
    pl.semaphore_wait(barrier, total - 1)
    lax.fori_loop(1, total, send, 0)
    lax.fori_loop(1, total, finish, 0)


def gather_all(block, sizes, collective_id):
    total = sizes[0] * sizes[1] * sizes[2]
    return pl.pallas_call(
        functools.partial(gather_kernel, sizes),
        out_shape=jax.ShapeDtypeStruct((total,) + block.shape, block.dtype),
        in_specs=[pl.BlockSpec(memory_space=pltpu.VMEM)],
        out_specs=pl.BlockSpec(memory_space=pltpu.VMEM),
        scratch_shapes=[pltpu.SemaphoreType.DMA((total,)), pltpu.SemaphoreType.DMA((total,))],
        compiler_params=pltpu.CompilerParams(collective_id=collective_id, has_side_effects=True),
        name=f"gather_{collective_id}",
    )(block)


def plane_rows(x_ref, y_ref):
    rows, width = x_ref.shape
    y_total = y_ref.shape[0]
    parts = []
    for row in range(rows):
        parts.append((x_ref[row : row + 1, :] * y_ref[...]).astype(jnp.bfloat16))
    return jnp.concatenate(parts, axis=0)


def potential_kernel(x_ref, y_ref, depth_ref, local_ref, out_ref):
    value = lax.dot_general(
        plane_rows(x_ref, y_ref),
        depth_ref[...],
        (((1,), (1,)), ((), ())),
        preferred_element_type=jnp.float32,
    )
    rounded = value.astype(jnp.bfloat16).astype(jnp.float32).reshape(out_ref.shape)
    out_ref[...] = local_ref[...].astype(jnp.float32) + rounded


def slab_potential(x_value, y_value, depth, v_local):
    x_total, y_total, z_total = v_local.shape
    width = x_value.shape[1]
    rows = 16
    return pl.pallas_call(
        potential_kernel,
        grid=(x_total // rows,),
        out_shape=jax.ShapeDtypeStruct(v_local.shape, jnp.float32),
        in_specs=[
            pl.BlockSpec((rows, width), lambda i: (i, 0)),
            pl.BlockSpec((y_total, width), lambda i: (0, 0)),
            pl.BlockSpec((z_total, width), lambda i: (0, 0)),
            pl.BlockSpec((rows, y_total, z_total), lambda i: (i, 0, 0)),
        ],
        out_specs=pl.BlockSpec((rows, y_total, z_total), lambda i: (i, 0, 0)),
        cost_estimate=pl.CostEstimate(
            flops=8 * x_total * y_total * z_total * width,
            bytes_accessed=6 * x_total * y_total * z_total,
            transcendentals=0,
        ),
        name="slab_potential",
    )(x_value, y_value, depth, v_local)


def force_kernel(xv_ref, xs_ref, yv_ref, ys_ref, real_ref, out_ref):
    @pl.when(pl.program_id(0) == 0)
    def _():
        out_ref[...] = jnp.zeros_like(out_ref)

    rows, y_total, z_total = real_ref.shape
    density = real_ref[...].astype(jnp.float32)
    density = (density * density).astype(jnp.bfloat16).reshape(rows * y_total, z_total)
    for part, (xr, yr) in enumerate(((xv_ref, yv_ref), (xs_ref, yv_ref), (xv_ref, ys_ref))):
        out_ref[part] += lax.dot_general(
            density,
            plane_rows(xr, yr),
            (((0,), (0,)), ((), ())),
            preferred_element_type=jnp.float32,
        )


def slab_moments(x_value, x_slope, y_value, y_slope, real_space):
    x_total, y_total, z_total = real_space.shape
    width = x_value.shape[1]
    rows = 16
    return pl.pallas_call(
        force_kernel,
        grid=(x_total // rows,),
        out_shape=jax.ShapeDtypeStruct((3, z_total, width), jnp.float32),
        in_specs=[
            pl.BlockSpec((rows, width), lambda i: (i, 0)),
            pl.BlockSpec((rows, width), lambda i: (i, 0)),
            pl.BlockSpec((y_total, width), lambda i: (0, 0)),
            pl.BlockSpec((y_total, width), lambda i: (0, 0)),
            pl.BlockSpec((rows, y_total, z_total), lambda i: (i, 0, 0)),
        ],
        out_specs=pl.BlockSpec((3, z_total, width), lambda i: (0, 0, 0)),
        cost_estimate=pl.CostEstimate(
            flops=12 * x_total * y_total * z_total * width,
            bytes_accessed=2 * x_total * y_total * z_total,
            transcendentals=0,
        ),
        name="slab_moments",
    )(x_value, x_slope, y_value, y_slope, real_space)


def per_device(sizes, coeffs, v_local, atom_pos, atom_charge, near_list, live_count):
    local_bands, x_local, extent, _ = coeffs.shape
    cosines = cosine_table(extent)
    gvec_id = lax.axis_index("gvec")
    group_id = lax.axis_index("band") * sizes[2] + lax.axis_index("dom")
    me = (lax.axis_index("band") * sizes[1] + gvec_id) * sizes[2] + lax.axis_index("dom")
    groups = sizes[0] * sizes[2]
    devices = groups * sizes[1]
    band_total = local_bands * groups
    cell_count = float(extent**3)
    band_ids = group_id * local_bands + jnp.arange(local_bands)
    weight = occupancy(band_ids, band_total)
    capacity = near_list.shape[0]
    live_mask = (jnp.arange(capacity) < live_count[0]).astype(jnp.float32)
    picked_pos = jnp.take(atom_pos, near_list, axis=1)
    picked_charge = jnp.take(atom_charge, near_list) * live_mask
    own_block = jnp.concatenate([picked_pos, picked_charge[None, :], live_mask[None, :]], axis=0)
    lanes = -(-capacity // 128) * 128
    tile = jnp.pad(own_block, ((0, 3), (0, lanes - capacity)))
    gathered = gather_all(tile, sizes, 0)
    coeffs, gathered = lax.optimization_barrier((coeffs, gathered))
    all_blocks = gathered[:, :5, :capacity].transpose(1, 0, 2).reshape(5, devices * capacity)
    live_total = all_blocks.shape[1] // 4
    order = jnp.cumsum(all_blocks[4]) - 1.0
    target = jnp.where(all_blocks[4] > 0.5, order, float(live_total)).astype(jnp.int32)
    select = (target[:, None] == jnp.arange(live_total)[None, :]).astype(jnp.float32)
    charges = jnp.dot(all_blocks[:4], select, precision=lax.Precision.HIGHEST)

    y_share = v_local.shape[1]
    x_points = jnp.arange(extent).astype(jnp.float32)
    y_points = (gvec_id * y_share + jnp.arange(y_share)).astype(jnp.float32)
    x_value, x_slope = kernels(x_points, charges[0], extent)
    y_value, y_slope = kernels(y_points, charges[1], extent)
    z_value, z_slope = kernels(x_points, charges[2], extent)
    weights = jnp.array(kernel_weights, jnp.float32)
    scaled = (weights[:, None] * charges[3][None, :]).reshape(-1)
    depth = (scaled[None, :] * z_value).astype(jnp.bfloat16)
    field_total = slab_potential(x_value, y_value, depth, v_local)

    gvec_size = sizes[1]
    chunks = 2 if y_share % 32 == 0 else 1
    chunk = y_share // chunks

    def y_rows(step, part):
        owner = lax.rem(gvec_id + step + gvec_size, gvec_size)
        return lax.dynamic_slice_in_dim(cosines, owner * y_share + part * chunk, chunk, 0)

    def a_columns(step):
        owner = lax.rem(gvec_id + step, gvec_size)
        return lax.dynamic_slice_in_dim(cosines, owner * x_local, x_local, 1)

    def shift(value, step):
        return lax.ppermute(
            value, "gvec", [(at, (at + step) % gvec_size) for at in range(gvec_size)]
        )

    section_z = jnp.einsum(
        "naql,zl->naqz", coeffs, cosines, preferred_element_type=jnp.float32
    ).astype(jnp.bfloat16)

    def section_y(step, part):
        return jnp.einsum(
            "naqz,yq->nayz", section_z, y_rows(step, part), preferred_element_type=jnp.float32
        ).astype(jnp.bfloat16)

    arrived = [
        [shift(section_y(-step, part), -step) for step in range(1, gvec_size)]
        for part in range(chunks)
    ]
    coeff_wide = coeffs.astype(jnp.float32)
    wave_step = jnp.pi / extent
    x_wave = (gvec_id * x_local + jnp.arange(x_local)).astype(jnp.float32) * wave_step
    y_wave = jnp.arange(extent).astype(jnp.float32) * wave_step
    kinetic = 0.5 * (
        x_wave[:, None, None] ** 2 + y_wave[None, :, None] ** 2 + y_wave[None, None, :] ** 2
    )
    norm_part = jnp.sum(coeff_wide * coeff_wide, axis=(1, 2, 3))
    weighted = jnp.sum(weight[:, None, None, None] * coeff_wide * coeff_wide, axis=0)
    stress_local = stress_terms(weighted, x_wave, y_wave) / cell_count

    moments = 0.0
    returned = []
    own_sections = [section_y(0, part) for part in range(chunks)]
    for part in range(chunks):
        window = slice(part * chunk, (part + 1) * chunk)
        held = [own_sections[part]] + arrived[part]
        real_space = sum(
            jnp.einsum("nayz,xa->nxyz", block, a_columns(step), preferred_element_type=jnp.float32)
            for step, block in enumerate(held)
        ).astype(jnp.bfloat16)
        applied = (field_total[None, :, window] * real_space.astype(jnp.float32)).astype(jnp.bfloat16)

        def back_x(step):
            return jnp.einsum(
                "nxyz,xa->nayz", applied, a_columns(step), preferred_element_type=jnp.float32
            ).astype(jnp.bfloat16)

        if part == chunks - 1:
            applied, stress_local, norm_part = lax.optimization_barrier(
                (applied, stress_local, norm_part)
            )
        returned.append([shift(back_x(step), step) for step in range(1, gvec_size)] + [back_x(0)])
        for band in range(local_bands):
            moments = moments + weight[band] * slab_moments(
                x_value, x_slope, y_value[window], y_slope[window], real_space[band]
            )
    embedding = jnp.sum(moments[0] * depth.astype(jnp.float32)) / cell_count
    force_terms = jnp.stack(
        [
            jnp.sum(moments[1] * z_value, axis=0),
            jnp.sum(moments[2] * z_value, axis=0),
            jnp.sum(moments[0] * z_slope, axis=0),
        ]
    )
    force_terms = force_terms * scaled[None, :]
    forces = -force_unit * jnp.sum(force_terms.reshape(3, len(kernel_weights), -1), axis=1)

    steps = list(range(-1, -gvec_size, -1)) + [0]
    back_two = sum(
        jnp.einsum("nayz,yq->naqz", block, y_rows(step, part), preferred_element_type=jnp.float32)
        for part in range(chunks)
        for step, block in zip(steps, returned[part])
    ).astype(jnp.bfloat16)
    wave_field = jnp.einsum("naqz,zl->naql", back_two, cosines, preferred_element_type=jnp.float32)
    image = kinetic[None] * coeff_wide + wave_field
    inner_part = jnp.sum(coeff_wide * image, axis=(1, 2, 3))
    own_energy = jnp.where(norm_part > 0.0, inner_part / jnp.where(norm_part > 0.0, norm_part, 1.0), 0.0)
    own_residual = image - own_energy[:, None, None, None] * coeff_wide
    resid_part = jnp.sum(own_residual * own_residual, axis=(1, 2, 3))
    local_totals = jnp.concatenate([stress_local, embedding[None]])
    mine = (jnp.arange(band_total)[None, :] == band_ids[:, None]).astype(jnp.float32)
    band_rows = jnp.stack([norm_part, inner_part, resid_part])
    flat = jnp.concatenate([forces.reshape(-1), local_totals])
    flat = jnp.pad(flat, (0, -flat.shape[0] % 128)).reshape(-1, 128)
    bands = jnp.pad(band_rows, ((0, -(flat.shape[0] + 3) % 8), (0, 128 - local_bands)))
    parts = gather_all(jnp.concatenate([flat, bands]), sizes, 1)
    lines = flat.shape[0]
    summed = jnp.sum(parts[:, :lines], axis=0).reshape(-1)
    force_all = summed[: 3 * live_total].reshape(3, live_total)
    by_group = parts[:, lines : lines + 3, :local_bands].reshape(
        sizes[0], gvec_size, sizes[2], 3, local_bands
    )
    norms, inners, squares = by_group[:, :, :, 0], by_group[:, :, :, 1], by_group[:, :, :, 2]
    norm_all = jnp.sum(norms, axis=1)
    energy_all = jnp.sum(inners, axis=1) / norm_all
    own_all = jnp.where(norms > 0.0, inners / jnp.where(norms > 0.0, norms, 1.0), 0.0)
    shifted = energy_all[:, None] - own_all
    ratio_all = (jnp.sum(squares + shifted * shifted * norms, axis=1) / norm_all).reshape(-1)
    energy_all = energy_all.reshape(-1)
    energies = jnp.sum(mine * energy_all[None, :], axis=1)
    resid_ratio = jnp.sum(mine * ratio_all[None, :], axis=1)
    residual = image - energies[:, None, None, None] * coeff_wide
    waves_new = (coeff_wide - step_size * residual / (1.0 + kinetic[None])).astype(jnp.bfloat16)
    band_energy = jnp.sum(occupancy(jnp.arange(band_total), band_total) * energy_all) / band_total
    totals = jnp.concatenate([summed[3 * live_total : 3 * live_total + 7], band_energy[None]])
    start = lax.dynamic_slice(order, (me * capacity,), (capacity,))
    own_target = jnp.where(live_mask > 0.5, start, float(live_total)).astype(jnp.int32)
    slot_select = (own_target[None, :] == jnp.arange(live_total)[:, None]).astype(jnp.float32)
    slot_force = jnp.dot(force_all, slot_select, precision=lax.Precision.HIGHEST)
    atom_select = (near_list[:, None] == jnp.arange(atom_pos.shape[1])[None, :]).astype(jnp.float32)
    atom_force = jnp.dot(slot_force, atom_select, precision=lax.Precision.HIGHEST)
    return (waves_new, energies, resid_ratio, atom_force, totals)


def solution(mesh):
    sizes = (mesh.shape["band"], mesh.shape["gvec"], mesh.shape["dom"])
    return jax.shard_map(
        functools.partial(per_device, sizes),
        mesh=mesh,
        in_specs=(
            P(("band", "dom"), "gvec", None, None),
            P(None, "gvec", None),
            P(None, ("band", "gvec", "dom")),
            P(("band", "gvec", "dom")),
            P(("band", "gvec", "dom")),
            P(("band", "gvec", "dom")),
        ),
        out_specs=(
            P(("band", "dom"), "gvec", None, None),
            P(("band", "dom")),
            P(("band", "dom")),
            P(None, ("band", "gvec", "dom")),
            P(),
        ),
        check_vma=False,
    )
```

```python
import jax
import jax.numpy as jnp
from jax import lax
from jax.experimental import pallas as pl
from jax.experimental.pallas import tpu as pltpu
from jax.sharding import PartitionSpec as P
import functools

sigma_fractions = (1.0 / 32.0, 1.0 / 16.0, 1.0 / 8.0, 1.0 / 4.0)
kernel_weights = (1.0, 0.5, 0.25, 0.125)
force_unit = 1.0 / 4096.0
step_size = 0.5


def cosine_table(length):
    points = jnp.arange(length).astype(jnp.float32)
    angles = jnp.pi * (points[:, None] + 0.5) * points[None, :] / length
    scales = jnp.where(points == 0.0, jnp.sqrt(1.0 / length), jnp.sqrt(2.0 / length))
    return (jnp.cos(angles) * scales[None, :]).astype(jnp.bfloat16)


def occupancy(band_index, band_total):
    shifted = band_index.astype(jnp.float32) - 0.5 * band_total
    return 2.0 / (1.0 + jnp.exp(shifted / (0.125 * band_total)))


def kernels(points, centres, extent):
    values = []
    slopes = []
    for fraction in sigma_fractions:
        exponent = 0.5 / (extent * fraction) ** 2
        offset = points[:, None] - centres[None, :]
        gauss_value = jnp.exp(-exponent * offset * offset)
        values.append(gauss_value)
        slopes.append(2.0 * exponent * offset * gauss_value)
    return (jnp.concatenate(values, axis=1), jnp.concatenate(slopes, axis=1))


def stress_terms(weighted, x_wave, y_wave):
    over_z = jnp.sum(weighted, axis=2)
    over_y = jnp.sum(weighted, axis=1)
    over_x = jnp.sum(weighted, axis=0)
    stress_xx = jnp.sum(x_wave * x_wave * jnp.sum(over_z, axis=1))
    stress_yy = jnp.sum(y_wave * y_wave * jnp.sum(over_z, axis=0))
    stress_zz = jnp.sum(y_wave * y_wave * jnp.sum(over_y, axis=0))
    stress_xy = jnp.sum(x_wave[:, None] * y_wave[None, :] * over_z)
    stress_xz = jnp.sum(x_wave[:, None] * y_wave[None, :] * over_y)
    stress_yz = jnp.sum(y_wave[:, None] * y_wave[None, :] * over_x)
    return jnp.stack([stress_xx, stress_yy, stress_zz, stress_xy, stress_xz, stress_yz])


def peer_coords(index, sizes):
    _, gvec_size, dom_size = sizes
    return (index // (gvec_size * dom_size), (index // dom_size) % gvec_size, index % dom_size)


def gather_kernel(sizes, x_ref, out_ref, send_sem, recv_sem):
    total = sizes[0] * sizes[1] * sizes[2]
    me = (lax.axis_index("band") * sizes[1] + lax.axis_index("gvec")) * sizes[2] + lax.axis_index("dom")
    barrier = pltpu.get_barrier_semaphore()

    def greet(step, carry):
        peer = lax.rem(me + step, total)
        pl.semaphore_signal(
            barrier, inc=1, device_id=peer_coords(peer, sizes), device_id_type=pl.DeviceIdType.MESH
        )
        return carry

    def copy_of(step):
        peer = lax.rem(me + step, total)
        return pltpu.make_async_remote_copy(
            src_ref=x_ref,
            dst_ref=out_ref.at[me],
            send_sem=send_sem.at[step],
            recv_sem=recv_sem.at[step],
            device_id=peer_coords(peer, sizes),
            device_id_type=pl.DeviceIdType.MESH,
        )

    def send(step, carry):
        copy_of(step).start()
        return carry

    def finish(step, carry):
        copy_of(step).wait()
        return carry

    lax.fori_loop(1, total, greet, 0)
    out_ref[me] = x_ref[...]
    pl.semaphore_wait(barrier, total - 1)
    lax.fori_loop(1, total, send, 0)
    lax.fori_loop(1, total, finish, 0)


def gather_all(block, sizes, collective_id):
    total = sizes[0] * sizes[1] * sizes[2]
    return pl.pallas_call(
        functools.partial(gather_kernel, sizes),
        out_shape=jax.ShapeDtypeStruct((total,) + block.shape, block.dtype),
        in_specs=[pl.BlockSpec(memory_space=pltpu.VMEM)],
        out_specs=pl.BlockSpec(memory_space=pltpu.VMEM),
        scratch_shapes=[pltpu.SemaphoreType.DMA((total,)), pltpu.SemaphoreType.DMA((total,))],
        compiler_params=pltpu.CompilerParams(collective_id=collective_id, has_side_effects=True),
        name=f"gather_{collective_id}",
    )(block)


def plane_rows(x_ref, y_ref):
    rows, width = x_ref.shape
    y_total = y_ref.shape[0]
    parts = []
    for row in range(rows):
        parts.append((x_ref[row : row + 1, :] * y_ref[...]).astype(jnp.bfloat16))
    return jnp.concatenate(parts, axis=0)


def potential_kernel(x_ref, y_ref, depth_ref, local_ref, out_ref):
    value = lax.dot_general(
        plane_rows(x_ref, y_ref),
        depth_ref[...],
        (((1,), (1,)), ((), ())),
        preferred_element_type=jnp.float32,
    )
    rounded = value.astype(jnp.bfloat16).astype(jnp.float32).reshape(out_ref.shape)
    out_ref[...] = local_ref[...].astype(jnp.float32) + rounded


def slab_potential(x_value, y_value, depth, v_local):
    x_total, y_total, z_total = v_local.shape
    width = x_value.shape[1]
    rows = 16
    return pl.pallas_call(
        potential_kernel,
        grid=(x_total // rows,),
        out_shape=jax.ShapeDtypeStruct(v_local.shape, jnp.float32),
        in_specs=[
            pl.BlockSpec((rows, width), lambda i: (i, 0)),
            pl.BlockSpec((y_total, width), lambda i: (0, 0)),
            pl.BlockSpec((z_total, width), lambda i: (0, 0)),
            pl.BlockSpec((rows, y_total, z_total), lambda i: (i, 0, 0)),
        ],
        out_specs=pl.BlockSpec((rows, y_total, z_total), lambda i: (i, 0, 0)),
        cost_estimate=pl.CostEstimate(
            flops=8 * x_total * y_total * z_total * width,
            bytes_accessed=6 * x_total * y_total * z_total,
            transcendentals=0,
        ),
        name="slab_potential",
    )(x_value, y_value, depth, v_local)


def force_kernel(xv_ref, xs_ref, yv_ref, ys_ref, real_ref, out_ref):
    @pl.when(pl.program_id(0) == 0)
    def _():
        out_ref[...] = jnp.zeros_like(out_ref)

    rows, y_total, z_total = real_ref.shape
    density = real_ref[...].astype(jnp.float32)
    density = (density * density).astype(jnp.bfloat16).reshape(rows * y_total, z_total)
    for part, (xr, yr) in enumerate(((xv_ref, yv_ref), (xs_ref, yv_ref), (xv_ref, ys_ref))):
        out_ref[part] += lax.dot_general(
            density,
            plane_rows(xr, yr),
            (((0,), (0,)), ((), ())),
            preferred_element_type=jnp.float32,
        )


def slab_moments(x_value, x_slope, y_value, y_slope, real_space):
    x_total, y_total, z_total = real_space.shape
    width = x_value.shape[1]
    rows = 16
    return pl.pallas_call(
        force_kernel,
        grid=(x_total // rows,),
        out_shape=jax.ShapeDtypeStruct((3, z_total, width), jnp.float32),
        in_specs=[
            pl.BlockSpec((rows, width), lambda i: (i, 0)),
            pl.BlockSpec((rows, width), lambda i: (i, 0)),
            pl.BlockSpec((y_total, width), lambda i: (0, 0)),
            pl.BlockSpec((y_total, width), lambda i: (0, 0)),
            pl.BlockSpec((rows, y_total, z_total), lambda i: (i, 0, 0)),
        ],
        out_specs=pl.BlockSpec((3, z_total, width), lambda i: (0, 0, 0)),
        cost_estimate=pl.CostEstimate(
            flops=12 * x_total * y_total * z_total * width,
            bytes_accessed=2 * x_total * y_total * z_total,
            transcendentals=0,
        ),
        name="slab_moments",
    )(x_value, x_slope, y_value, y_slope, real_space)


def per_device(sizes, coeffs, v_local, atom_pos, atom_charge, near_list, live_count):
    local_bands, x_local, extent, _ = coeffs.shape
    cosines = cosine_table(extent)
    gvec_id = lax.axis_index("gvec")
    group_id = lax.axis_index("band") * sizes[2] + lax.axis_index("dom")
    me = (lax.axis_index("band") * sizes[1] + gvec_id) * sizes[2] + lax.axis_index("dom")
    groups = sizes[0] * sizes[2]
    devices = groups * sizes[1]
    band_total = local_bands * groups
    cell_count = float(extent**3)
    band_ids = group_id * local_bands + jnp.arange(local_bands)
    weight = occupancy(band_ids, band_total)
    capacity = near_list.shape[0]
    live_mask = (jnp.arange(capacity) < live_count[0]).astype(jnp.float32)
    picked_pos = jnp.take(atom_pos, near_list, axis=1)
    picked_charge = jnp.take(atom_charge, near_list) * live_mask
    own_block = jnp.concatenate([picked_pos, picked_charge[None, :], live_mask[None, :]], axis=0)
    lanes = -(-capacity // 128) * 128
    tile = jnp.pad(own_block, ((0, 3), (0, lanes - capacity)))
    gathered = gather_all(tile, sizes, 0)
    coeffs, gathered = lax.optimization_barrier((coeffs, gathered))
    all_blocks = gathered[:, :5, :capacity].transpose(1, 0, 2).reshape(5, devices * capacity)
    live_total = all_blocks.shape[1] // 4
    order = jnp.cumsum(all_blocks[4]) - 1.0
    target = jnp.where(all_blocks[4] > 0.5, order, float(live_total)).astype(jnp.int32)
    select = (target[:, None] == jnp.arange(live_total)[None, :]).astype(jnp.float32)
    charges = jnp.dot(all_blocks[:4], select, precision=lax.Precision.HIGHEST)

    y_share = v_local.shape[1]
    x_points = jnp.arange(extent).astype(jnp.float32)
    y_points = (gvec_id * y_share + jnp.arange(y_share)).astype(jnp.float32)
    x_value, x_slope = kernels(x_points, charges[0], extent)
    y_value, y_slope = kernels(y_points, charges[1], extent)
    z_value, z_slope = kernels(x_points, charges[2], extent)
    weights = jnp.array(kernel_weights, jnp.float32)
    scaled = (weights[:, None] * charges[3][None, :]).reshape(-1)
    depth = (scaled[None, :] * z_value).astype(jnp.bfloat16)
    field_total = slab_potential(x_value, y_value, depth, v_local)

    gvec_size = sizes[1]
    chunks = 2 if y_share % 32 == 0 else 1
    chunk = y_share // chunks

    def y_rows(step, part):
        owner = lax.rem(gvec_id + step + gvec_size, gvec_size)
        return lax.dynamic_slice_in_dim(cosines, owner * y_share + part * chunk, chunk, 0)

    def a_columns(step):
        owner = lax.rem(gvec_id + step, gvec_size)
        return lax.dynamic_slice_in_dim(cosines, owner * x_local, x_local, 1)

    def shift(value, step):
        return lax.ppermute(
            value, "gvec", [(at, (at + step) % gvec_size) for at in range(gvec_size)]
        )

    section_z = jnp.einsum(
        "naql,zl->naqz", coeffs, cosines, preferred_element_type=jnp.float32
    ).astype(jnp.bfloat16)

    def section_y(step, part):
        return jnp.einsum(
            "naqz,yq->nayz", section_z, y_rows(step, part), preferred_element_type=jnp.float32
        ).astype(jnp.bfloat16)

    arrived = [
        [shift(section_y(-step, part), -step) for step in range(1, gvec_size)]
        for part in range(chunks)
    ]
    moments = 0.0
    reals = []
    returned = []
    own_sections = [section_y(0, part) for part in range(chunks)]
    for part in range(chunks):
        window = slice(part * chunk, (part + 1) * chunk)
        held = [own_sections[part]] + arrived[part]
        real_space = sum(
            jnp.einsum("nayz,xa->nxyz", block, a_columns(step), preferred_element_type=jnp.float32)
            for step, block in enumerate(held)
        ).astype(jnp.bfloat16)
        applied = (field_total[None, :, window] * real_space.astype(jnp.float32)).astype(jnp.bfloat16)

        def back_x(step):
            return jnp.einsum(
                "nxyz,xa->nayz", applied, a_columns(step), preferred_element_type=jnp.float32
            ).astype(jnp.bfloat16)

        sent = [back_x(step) for step in range(1, gvec_size)]
        if part == chunks - 1:
            sent, held_coeffs, reals = lax.optimization_barrier(
                (sent, coeffs, reals + [real_space])
            )
        else:
            reals.append(real_space)
        returned.append(
            [shift(block, step) for step, block in enumerate(sent, 1)] + [back_x(0)]
        )
    for part in range(chunks):
        window = slice(part * chunk, (part + 1) * chunk)
        for band in range(local_bands):
            moments = moments + weight[band] * slab_moments(
                x_value, x_slope, y_value[window], y_slope[window], reals[part][band]
            )
    coeff_wide = held_coeffs.astype(jnp.float32)
    wave_step = jnp.pi / extent
    x_wave = (gvec_id * x_local + jnp.arange(x_local)).astype(jnp.float32) * wave_step
    y_wave = jnp.arange(extent).astype(jnp.float32) * wave_step
    kinetic = 0.5 * (
        x_wave[:, None, None] ** 2 + y_wave[None, :, None] ** 2 + y_wave[None, None, :] ** 2
    )
    norm_part = jnp.sum(coeff_wide * coeff_wide, axis=(1, 2, 3))
    weighted = jnp.sum(weight[:, None, None, None] * coeff_wide * coeff_wide, axis=0)
    stress_local = stress_terms(weighted, x_wave, y_wave) / cell_count

    embedding = jnp.sum(moments[0] * depth.astype(jnp.float32)) / cell_count
    force_terms = jnp.stack(
        [
            jnp.sum(moments[1] * z_value, axis=0),
            jnp.sum(moments[2] * z_value, axis=0),
            jnp.sum(moments[0] * z_slope, axis=0),
        ]
    )
    force_terms = force_terms * scaled[None, :]
    forces = -force_unit * jnp.sum(force_terms.reshape(3, len(kernel_weights), -1), axis=1)

    steps = list(range(-1, -gvec_size, -1)) + [0]
    back_two = sum(
        jnp.einsum("nayz,yq->naqz", block, y_rows(step, part), preferred_element_type=jnp.float32)
        for part in range(chunks)
        for step, block in zip(steps, returned[part])
    ).astype(jnp.bfloat16)
    wave_field = jnp.einsum("naqz,zl->naql", back_two, cosines, preferred_element_type=jnp.float32)
    image = kinetic[None] * coeff_wide + wave_field
    inner_part = jnp.sum(coeff_wide * image, axis=(1, 2, 3))
    own_energy = jnp.where(norm_part > 0.0, inner_part / jnp.where(norm_part > 0.0, norm_part, 1.0), 0.0)
    own_residual = image - own_energy[:, None, None, None] * coeff_wide
    resid_part = jnp.sum(own_residual * own_residual, axis=(1, 2, 3))
    local_totals = jnp.concatenate([stress_local, embedding[None]])
    mine = (jnp.arange(band_total)[None, :] == band_ids[:, None]).astype(jnp.float32)
    flat = jnp.concatenate([forces.reshape(-1), local_totals, norm_part, inner_part, resid_part])
    flat = jnp.pad(flat, (0, -flat.shape[0] % 1024)).reshape(-1, 128)
    parts = gather_all(flat, sizes, 1).reshape(devices, -1)
    lines = 3 * live_total + 7
    summed = jnp.sum(parts[:, :lines], axis=0)
    force_all = summed[: 3 * live_total].reshape(3, live_total)
    by_group = parts[:, lines : lines + 3 * local_bands].reshape(
        sizes[0], gvec_size, sizes[2], 3, local_bands
    )
    norms, inners, squares = by_group[:, :, :, 0], by_group[:, :, :, 1], by_group[:, :, :, 2]
    norm_all = jnp.sum(norms, axis=1)
    energy_all = jnp.sum(inners, axis=1) / norm_all
    own_all = jnp.where(norms > 0.0, inners / jnp.where(norms > 0.0, norms, 1.0), 0.0)
    shifted = energy_all[:, None] - own_all
    ratio_all = (jnp.sum(squares + shifted * shifted * norms, axis=1) / norm_all).reshape(-1)
    energy_all = energy_all.reshape(-1)
    energies = jnp.sum(mine * energy_all[None, :], axis=1)
    resid_ratio = jnp.sum(mine * ratio_all[None, :], axis=1)
    residual = image - energies[:, None, None, None] * coeff_wide
    waves_new = (coeff_wide - step_size * residual / (1.0 + kinetic[None])).astype(jnp.bfloat16)
    band_energy = jnp.sum(occupancy(jnp.arange(band_total), band_total) * energy_all) / band_total
    totals = jnp.concatenate([summed[3 * live_total : 3 * live_total + 7], band_energy[None]])
    start = lax.dynamic_slice(order, (me * capacity,), (capacity,))
    own_target = jnp.where(live_mask > 0.5, start, float(live_total)).astype(jnp.int32)
    slot_select = (own_target[None, :] == jnp.arange(live_total)[:, None]).astype(jnp.float32)
    slot_force = jnp.dot(force_all, slot_select, precision=lax.Precision.HIGHEST)
    atom_select = (near_list[:, None] == jnp.arange(atom_pos.shape[1])[None, :]).astype(jnp.float32)
    atom_force = jnp.dot(slot_force, atom_select, precision=lax.Precision.HIGHEST)
    return (waves_new, energies, resid_ratio, atom_force, totals)


def solution(mesh):
    sizes = (mesh.shape["band"], mesh.shape["gvec"], mesh.shape["dom"])
    return jax.shard_map(
        functools.partial(per_device, sizes),
        mesh=mesh,
        in_specs=(
            P(("band", "dom"), "gvec", None, None),
            P(None, "gvec", None),
            P(None, ("band", "gvec", "dom")),
            P(("band", "gvec", "dom")),
            P(("band", "gvec", "dom")),
            P(("band", "gvec", "dom")),
        ),
        out_specs=(
            P(("band", "dom"), "gvec", None, None),
            P(("band", "dom")),
            P(("band", "dom")),
            P(None, ("band", "gvec", "dom")),
            P(),
        ),
        check_vma=False,
    )
```

```python
import jax
import jax.numpy as jnp
from jax import lax
from jax.experimental import pallas as pl
from jax.experimental.pallas import tpu as pltpu
from jax.sharding import PartitionSpec as P
import functools

sigma_fractions = (1.0 / 32.0, 1.0 / 16.0, 1.0 / 8.0, 1.0 / 4.0)
kernel_weights = (1.0, 0.5, 0.25, 0.125)
force_unit = 1.0 / 4096.0
step_size = 0.5


def cosine_table(length):
    points = jnp.arange(length).astype(jnp.float32)
    angles = jnp.pi * (points[:, None] + 0.5) * points[None, :] / length
    scales = jnp.where(points == 0.0, jnp.sqrt(1.0 / length), jnp.sqrt(2.0 / length))
    return (jnp.cos(angles) * scales[None, :]).astype(jnp.bfloat16)


def occupancy(band_index, band_total):
    shifted = band_index.astype(jnp.float32) - 0.5 * band_total
    return 2.0 / (1.0 + jnp.exp(shifted / (0.125 * band_total)))


def kernels(points, centres, extent):
    values = []
    slopes = []
    for fraction in sigma_fractions:
        exponent = 0.5 / (extent * fraction) ** 2
        offset = points[:, None] - centres[None, :]
        gauss_value = jnp.exp(-exponent * offset * offset)
        values.append(gauss_value)
        slopes.append(2.0 * exponent * offset * gauss_value)
    return (jnp.concatenate(values, axis=1), jnp.concatenate(slopes, axis=1))


def peer_coords(index, sizes):
    _, gvec_size, dom_size = sizes
    return (index // (gvec_size * dom_size), (index // dom_size) % gvec_size, index % dom_size)


def gather_kernel(sizes, x_ref, out_ref, send_sem, recv_sem):
    total = sizes[0] * sizes[1] * sizes[2]
    me = (lax.axis_index("band") * sizes[1] + lax.axis_index("gvec")) * sizes[2] + lax.axis_index("dom")
    barrier = pltpu.get_barrier_semaphore()

    def greet(step, carry):
        peer = lax.rem(me + step, total)
        pl.semaphore_signal(
            barrier, inc=1, device_id=peer_coords(peer, sizes), device_id_type=pl.DeviceIdType.MESH
        )
        return carry

    def copy_of(step):
        peer = lax.rem(me + step, total)
        return pltpu.make_async_remote_copy(
            src_ref=x_ref,
            dst_ref=out_ref.at[me],
            send_sem=send_sem.at[step],
            recv_sem=recv_sem.at[step],
            device_id=peer_coords(peer, sizes),
            device_id_type=pl.DeviceIdType.MESH,
        )

    def send(step, carry):
        copy_of(step).start()
        return carry

    def finish(step, carry):
        copy_of(step).wait()
        return carry

    lax.fori_loop(1, total, greet, 0)
    out_ref[me] = x_ref[...]
    pl.semaphore_wait(barrier, total - 1)
    lax.fori_loop(1, total, send, 0)
    lax.fori_loop(1, total, finish, 0)


def gather_all(block, sizes, collective_id):
    total = sizes[0] * sizes[1] * sizes[2]
    return pl.pallas_call(
        functools.partial(gather_kernel, sizes),
        out_shape=jax.ShapeDtypeStruct((total,) + block.shape, block.dtype),
        in_specs=[pl.BlockSpec(memory_space=pltpu.VMEM)],
        out_specs=pl.BlockSpec(memory_space=pltpu.VMEM),
        scratch_shapes=[pltpu.SemaphoreType.DMA((total,)), pltpu.SemaphoreType.DMA((total,))],
        compiler_params=pltpu.CompilerParams(collective_id=collective_id, has_side_effects=True),
        name=f"gather_{collective_id}",
    )(block)


def plane_rows(x_ref, y_ref):
    rows, width = x_ref.shape
    y_total = y_ref.shape[0]
    parts = []
    for row in range(rows):
        parts.append((x_ref[row : row + 1, :] * y_ref[...]).astype(jnp.bfloat16))
    return jnp.concatenate(parts, axis=0)


def potential_kernel(x_ref, y_ref, depth_ref, local_ref, out_ref):
    value = lax.dot_general(
        plane_rows(x_ref, y_ref),
        depth_ref[...],
        (((1,), (1,)), ((), ())),
        preferred_element_type=jnp.float32,
    )
    rounded = value.astype(jnp.bfloat16).astype(jnp.float32).reshape(out_ref.shape)
    out_ref[...] = local_ref[...].astype(jnp.float32) + rounded


def slab_potential(x_value, y_value, depth, v_local):
    x_total, y_total, z_total = v_local.shape
    width = x_value.shape[1]
    rows = 16
    return pl.pallas_call(
        potential_kernel,
        grid=(x_total // rows,),
        out_shape=jax.ShapeDtypeStruct(v_local.shape, jnp.float32),
        in_specs=[
            pl.BlockSpec((rows, width), lambda i: (i, 0)),
            pl.BlockSpec((y_total, width), lambda i: (0, 0)),
            pl.BlockSpec((z_total, width), lambda i: (0, 0)),
            pl.BlockSpec((rows, y_total, z_total), lambda i: (i, 0, 0)),
        ],
        out_specs=pl.BlockSpec((rows, y_total, z_total), lambda i: (i, 0, 0)),
        cost_estimate=pl.CostEstimate(
            flops=8 * x_total * y_total * z_total * width,
            bytes_accessed=6 * x_total * y_total * z_total,
            transcendentals=0,
        ),
        name="slab_potential",
    )(x_value, y_value, depth, v_local)


def force_kernel(xv_ref, xs_ref, yv_ref, ys_ref, real_ref, out_ref):
    @pl.when(pl.program_id(0) == 0)
    def _():
        out_ref[...] = jnp.zeros_like(out_ref)

    rows, y_total, z_total = real_ref.shape
    density = real_ref[...].astype(jnp.float32)
    density = (density * density).astype(jnp.bfloat16).reshape(rows * y_total, z_total)
    for part, (xr, yr) in enumerate(((xv_ref, yv_ref), (xs_ref, yv_ref), (xv_ref, ys_ref))):
        out_ref[part] += lax.dot_general(
            density,
            plane_rows(xr, yr),
            (((0,), (0,)), ((), ())),
            preferred_element_type=jnp.float32,
        )


def slab_moments(x_value, x_slope, y_value, y_slope, real_space):
    x_total, y_total, z_total = real_space.shape
    width = x_value.shape[1]
    rows = 16
    return pl.pallas_call(
        force_kernel,
        grid=(x_total // rows,),
        out_shape=jax.ShapeDtypeStruct((3, z_total, width), jnp.float32),
        in_specs=[
            pl.BlockSpec((rows, width), lambda i: (i, 0)),
            pl.BlockSpec((rows, width), lambda i: (i, 0)),
            pl.BlockSpec((y_total, width), lambda i: (0, 0)),
            pl.BlockSpec((y_total, width), lambda i: (0, 0)),
            pl.BlockSpec((rows, y_total, z_total), lambda i: (i, 0, 0)),
        ],
        out_specs=pl.BlockSpec((3, z_total, width), lambda i: (0, 0, 0)),
        cost_estimate=pl.CostEstimate(
            flops=12 * x_total * y_total * z_total * width,
            bytes_accessed=2 * x_total * y_total * z_total,
            transcendentals=0,
        ),
        name="slab_moments",
    )(x_value, x_slope, y_value, y_slope, real_space)


def tail_kernel(
    sizes, base, back_ref, coeff_ref, table_ref, weight_ref, head_ref,
    waves_ref, out_ref, image_ref, sums_ref, tile_ref, send_sem, recv_sem,
):
    band_size, gvec_size, dom_size = sizes
    total = band_size * gvec_size * dom_size
    band_id, gvec_id, dom_id = lax.axis_index("band"), lax.axis_index("gvec"), lax.axis_index("dom")
    me = (band_id * gvec_size + gvec_id) * dom_size + dom_id
    local_bands, x_local, extent, _ = coeff_ref.shape
    barrier = pltpu.get_barrier_semaphore()

    def peer_of(step):
        outer = step // gvec_size
        return (
            lax.rem(band_id + outer // dom_size, band_size),
            lax.rem(gvec_id + step % gvec_size, gvec_size),
            lax.rem(dom_id + outer % dom_size, dom_size),
        )

    def greet(step, carry):
        pl.semaphore_signal(
            barrier, inc=1, device_id=peer_of(step), device_id_type=pl.DeviceIdType.MESH
        )
        return carry

    lax.fori_loop(1, total, greet, 0)

    def copy_of(step):
        return pltpu.make_async_remote_copy(
            src_ref=tile_ref,
            dst_ref=out_ref.at[me],
            send_sem=send_sem.at[step],
            recv_sem=recv_sem.at[step],
            device_id=peer_of(step),
            device_id_type=pl.DeviceIdType.MESH,
        )

    def send(step, carry):
        copy_of(step).start()
        return carry

    def finish(step, carry):
        copy_of(step).wait()
        return carry

    rows = 4
    block = (rows, extent, extent)
    wave_step = jnp.pi / extent
    q_wave = lax.broadcasted_iota(jnp.int32, block[1:], 0).astype(jnp.float32) * wave_step
    l_wave = lax.broadcasted_iota(jnp.int32, block[1:], 1).astype(jnp.float32) * wave_step
    plane_kinetic = 0.5 * (q_wave * q_wave + l_wave * l_wave)

    def x_waves(index):
        first = gvec_id * x_local + index * rows
        at = lax.broadcasted_iota(jnp.int32, block, 0) + first
        return at.astype(jnp.float32) * wave_step

    def total_of(value):
        return jnp.sum(jnp.sum(value, axis=0, keepdims=True), axis=1, keepdims=True)

    spots = (
        lax.broadcasted_iota(jnp.int32, head_ref.shape, 0) * 128
        + lax.broadcasted_iota(jnp.int32, head_ref.shape, 1)
    )
    tile = head_ref[...]
    stress = [0.0] * 6
    for band in range(local_bands):
        sums_ref[...] = jnp.zeros_like(sums_ref)

        def first_pass(index, carry):
            window = pl.ds(index * rows, rows)
            wide = coeff_ref[band, window].astype(jnp.float32)
            field = jnp.dot(
                back_ref[band, window].reshape(rows * extent, extent),
                table_ref[...],
                preferred_element_type=jnp.float32,
            ).reshape(block)
            x_wave = x_waves(index)
            image = (0.5 * x_wave * x_wave + plane_kinetic[None]) * wide + field
            image_ref[band, window] = image
            square = wide * wide
            by_x = square * x_wave
            sums_ref[0] += jnp.sum(square, axis=0)
            sums_ref[1] += jnp.sum(by_x, axis=0)
            sums_ref[2] += jnp.sum(by_x * x_wave, axis=0)
            sums_ref[3] += jnp.sum(wide * image, axis=0)
            return carry

        lax.fori_loop(0, x_local // rows, first_pass, 0)
        norm = total_of(sums_ref[0])
        inner = total_of(sums_ref[3])
        filled = norm > 0.0
        energy = jnp.where(filled, inner / jnp.where(filled, norm, 1.0), 0.0)
        weight = weight_ref[0:1, band : band + 1]
        terms = (
            sums_ref[2],
            sums_ref[0] * q_wave * q_wave,
            sums_ref[0] * l_wave * l_wave,
            sums_ref[1] * q_wave,
            sums_ref[1] * l_wave,
            sums_ref[0] * q_wave * l_wave,
        )
        stress = [old + weight * total_of(term) for old, term in zip(stress, terms)]
        sums_ref[1] = jnp.zeros_like(sums_ref[1])

        def second_pass(index, carry):
            window = pl.ds(index * rows, rows)
            wide = coeff_ref[band, window].astype(jnp.float32)
            residual = image_ref[band, window] - energy[None] * wide
            sums_ref[1] += jnp.sum(residual * residual, axis=0)
            return carry

        lax.fori_loop(0, x_local // rows, second_pass, 0)
        square = total_of(sums_ref[1])
        for shift, value in enumerate((norm, inner, square)):
            tile = jnp.where(spots == base + 7 + shift * local_bands + band, value, tile)
    for shift, value in enumerate(stress):
        tile = jnp.where(spots == base + shift, value / float(extent**3), tile)
    tile_ref[...] = tile
    out_ref[me] = tile
    pl.semaphore_wait(barrier, total - 1)
    lax.fori_loop(1, total, send, 0)
    lax.fori_loop(1, gvec_size, finish, 0)

    both = tile
    for step in range(1, gvec_size):
        other = lax.rem(gvec_id + step, gvec_size)
        both = both + out_ref[(band_id * gvec_size + other) * dom_size + dom_id]
    for band in range(local_bands):
        norm = total_of(jnp.where(spots == base + 7 + band, both, 0.0))
        inner = total_of(jnp.where(spots == base + 7 + local_bands + band, both, 0.0))
        energy = inner / norm

        def last_pass(index, carry):
            window = pl.ds(index * rows, rows)
            wide = coeff_ref[band, window].astype(jnp.float32)
            x_wave = x_waves(index)
            kinetic = 0.5 * x_wave * x_wave + plane_kinetic[None]
            residual = image_ref[band, window] - energy[None] * wide
            updated = wide - step_size * residual / (1.0 + kinetic)
            waves_ref[band, window] = updated.astype(jnp.bfloat16)
            return carry

        lax.fori_loop(0, x_local // rows, last_pass, 0)
    lax.fori_loop(gvec_size, total, finish, 0)


def tail(back_two, coeffs, cosines, weight, head, base, sizes):
    total = sizes[0] * sizes[1] * sizes[2]
    extent = coeffs.shape[-1]
    vmem = pl.BlockSpec(memory_space=pltpu.VMEM)
    return pl.pallas_call(
        functools.partial(tail_kernel, sizes, base),
        out_shape=(
            jax.ShapeDtypeStruct(coeffs.shape, jnp.bfloat16),
            jax.ShapeDtypeStruct((total,) + head.shape, jnp.float32),
        ),
        in_specs=[vmem] * 5,
        out_specs=(vmem, vmem),
        scratch_shapes=[
            pltpu.VMEM(coeffs.shape, jnp.float32),
            pltpu.VMEM((4, extent, extent), jnp.float32),
            pltpu.VMEM(head.shape, jnp.float32),
            pltpu.SemaphoreType.DMA((total,)),
            pltpu.SemaphoreType.DMA((total,)),
        ],
        compiler_params=pltpu.CompilerParams(
            collective_id=1, has_side_effects=True, vmem_limit_bytes=40 * 1024 * 1024
        ),
        name="tail",
    )(back_two, coeffs, cosines, weight, head)


def per_device(sizes, coeffs, v_local, atom_pos, atom_charge, near_list, live_count):
    local_bands, x_local, extent, _ = coeffs.shape
    cosines = cosine_table(extent)
    gvec_id = lax.axis_index("gvec")
    group_id = lax.axis_index("band") * sizes[2] + lax.axis_index("dom")
    me = (lax.axis_index("band") * sizes[1] + gvec_id) * sizes[2] + lax.axis_index("dom")
    groups = sizes[0] * sizes[2]
    devices = groups * sizes[1]
    band_total = local_bands * groups
    cell_count = float(extent**3)
    band_ids = group_id * local_bands + jnp.arange(local_bands)
    weight = occupancy(band_ids, band_total)
    capacity = near_list.shape[0]
    live_mask = (jnp.arange(capacity) < live_count[0]).astype(jnp.float32)
    picked_pos = jnp.take(atom_pos, near_list, axis=1)
    picked_charge = jnp.take(atom_charge, near_list) * live_mask
    own_block = jnp.concatenate([picked_pos, picked_charge[None, :], live_mask[None, :]], axis=0)
    lanes = -(-capacity // 128) * 128
    tile = jnp.pad(own_block, ((0, 3), (0, lanes - capacity)))
    gathered = gather_all(tile, sizes, 0)
    coeffs, gathered = lax.optimization_barrier((coeffs, gathered))
    all_blocks = gathered[:, :5, :capacity].transpose(1, 0, 2).reshape(5, devices * capacity)
    live_total = all_blocks.shape[1] // 4
    order = jnp.cumsum(all_blocks[4]) - 1.0
    target = jnp.where(all_blocks[4] > 0.5, order, float(live_total)).astype(jnp.int32)
    select = (target[:, None] == jnp.arange(live_total)[None, :]).astype(jnp.float32)
    charges = jnp.dot(all_blocks[:4], select, precision=lax.Precision.HIGHEST)

    y_share = v_local.shape[1]
    x_points = jnp.arange(extent).astype(jnp.float32)
    y_points = (gvec_id * y_share + jnp.arange(y_share)).astype(jnp.float32)
    x_value, x_slope = kernels(x_points, charges[0], extent)
    y_value, y_slope = kernels(y_points, charges[1], extent)
    z_value, z_slope = kernels(x_points, charges[2], extent)
    weights = jnp.array(kernel_weights, jnp.float32)
    scaled = (weights[:, None] * charges[3][None, :]).reshape(-1)
    depth = (scaled[None, :] * z_value).astype(jnp.bfloat16)
    field_total = slab_potential(x_value, y_value, depth, v_local)

    gvec_size = sizes[1]
    chunks = 2 if y_share % 32 == 0 else 1
    chunk = y_share // chunks

    def y_rows(step, part):
        owner = lax.rem(gvec_id + step + gvec_size, gvec_size)
        return lax.dynamic_slice_in_dim(cosines, owner * y_share + part * chunk, chunk, 0)

    def a_columns(step):
        owner = lax.rem(gvec_id + step, gvec_size)
        return lax.dynamic_slice_in_dim(cosines, owner * x_local, x_local, 1)

    def shift(value, step):
        return lax.ppermute(
            value, "gvec", [(at, (at + step) % gvec_size) for at in range(gvec_size)]
        )

    section_z = jnp.einsum(
        "naql,zl->naqz", coeffs, cosines, preferred_element_type=jnp.float32
    ).astype(jnp.bfloat16)

    def section_y(step, part):
        return jnp.einsum(
            "naqz,yq->nayz", section_z, y_rows(step, part), preferred_element_type=jnp.float32
        ).astype(jnp.bfloat16)

    arrived = [
        [shift(section_y(-step, part), -step) for step in range(1, gvec_size)]
        for part in range(chunks)
    ]
    moments = 0.0
    reals = []
    returned = []
    own_sections = [section_y(0, part) for part in range(chunks)]
    for part in range(chunks):
        window = slice(part * chunk, (part + 1) * chunk)
        held = [own_sections[part]] + arrived[part]
        real_space = sum(
            jnp.einsum("nayz,xa->nxyz", block, a_columns(step), preferred_element_type=jnp.float32)
            for step, block in enumerate(held)
        ).astype(jnp.bfloat16)
        applied = (field_total[None, :, window] * real_space.astype(jnp.float32)).astype(jnp.bfloat16)

        def back_x(step):
            return jnp.einsum(
                "nxyz,xa->nayz", applied, a_columns(step), preferred_element_type=jnp.float32
            ).astype(jnp.bfloat16)

        sent = [back_x(step) for step in range(1, gvec_size)]
        if part == chunks - 1:
            sent, reals = lax.optimization_barrier((sent, reals + [real_space]))
        else:
            reals.append(real_space)
        returned.append(
            [shift(block, step) for step, block in enumerate(sent, 1)] + [back_x(0)]
        )
    for part in range(chunks):
        window = slice(part * chunk, (part + 1) * chunk)
        for band in range(local_bands):
            moments = moments + weight[band] * slab_moments(
                x_value, x_slope, y_value[window], y_slope[window], reals[part][band]
            )
    embedding = jnp.sum(moments[0] * depth.astype(jnp.float32)) / cell_count
    force_terms = jnp.stack(
        [
            jnp.sum(moments[1] * z_value, axis=0),
            jnp.sum(moments[2] * z_value, axis=0),
            jnp.sum(moments[0] * z_slope, axis=0),
        ]
    )
    force_terms = force_terms * scaled[None, :]
    forces = -force_unit * jnp.sum(force_terms.reshape(3, len(kernel_weights), -1), axis=1)

    steps = list(range(-1, -gvec_size, -1)) + [0]
    back_two = sum(
        jnp.einsum("nayz,yq->naqz", block, y_rows(step, part), preferred_element_type=jnp.float32)
        for part in range(chunks)
        for step, block in zip(steps, returned[part])
    ).astype(jnp.bfloat16)
    mine = (jnp.arange(band_total)[None, :] == band_ids[:, None]).astype(jnp.float32)
    flat = jnp.concatenate([forces.reshape(-1), jnp.zeros((6,), jnp.float32), embedding[None]])
    tail_length = flat.shape[0] + 3 * local_bands
    flat = jnp.pad(flat, (0, 3 * local_bands + -tail_length % 1024)).reshape(-1, 128)
    weight_row = jnp.pad(weight, (0, -local_bands % 128))[None, :]
    waves_new, parts = tail(back_two, coeffs, cosines, weight_row, flat, 3 * live_total, sizes)
    parts = parts.reshape(devices, -1)
    lines = 3 * live_total + 7
    summed = jnp.sum(parts[:, :lines], axis=0)
    force_all = summed[: 3 * live_total].reshape(3, live_total)
    by_group = parts[:, lines : lines + 3 * local_bands].reshape(
        sizes[0], gvec_size, sizes[2], 3, local_bands
    )
    norms, inners, squares = by_group[:, :, :, 0], by_group[:, :, :, 1], by_group[:, :, :, 2]
    norm_all = jnp.sum(norms, axis=1)
    energy_all = jnp.sum(inners, axis=1) / norm_all
    own_all = jnp.where(norms > 0.0, inners / jnp.where(norms > 0.0, norms, 1.0), 0.0)
    shifted = energy_all[:, None] - own_all
    ratio_all = (jnp.sum(squares + shifted * shifted * norms, axis=1) / norm_all).reshape(-1)
    energy_all = energy_all.reshape(-1)
    energies = jnp.sum(mine * energy_all[None, :], axis=1)
    resid_ratio = jnp.sum(mine * ratio_all[None, :], axis=1)
    band_energy = jnp.sum(occupancy(jnp.arange(band_total), band_total) * energy_all) / band_total
    totals = jnp.concatenate([summed[3 * live_total : 3 * live_total + 7], band_energy[None]])
    start = lax.dynamic_slice(order, (me * capacity,), (capacity,))
    own_target = jnp.where(live_mask > 0.5, start, float(live_total)).astype(jnp.int32)
    slot_select = (own_target[None, :] == jnp.arange(live_total)[:, None]).astype(jnp.float32)
    slot_force = jnp.dot(force_all, slot_select, precision=lax.Precision.HIGHEST)
    atom_select = (near_list[:, None] == jnp.arange(atom_pos.shape[1])[None, :]).astype(jnp.float32)
    atom_force = jnp.dot(slot_force, atom_select, precision=lax.Precision.HIGHEST)
    return (waves_new, energies, resid_ratio, atom_force, totals)


def solution(mesh):
    sizes = (mesh.shape["band"], mesh.shape["gvec"], mesh.shape["dom"])
    return jax.shard_map(
        functools.partial(per_device, sizes),
        mesh=mesh,
        in_specs=(
            P(("band", "dom"), "gvec", None, None),
            P(None, "gvec", None),
            P(None, ("band", "gvec", "dom")),
            P(("band", "gvec", "dom")),
            P(("band", "gvec", "dom")),
            P(("band", "gvec", "dom")),
        ),
        out_specs=(
            P(("band", "dom"), "gvec", None, None),
            P(("band", "dom")),
            P(("band", "dom")),
            P(None, ("band", "gvec", "dom")),
            P(),
        ),
        check_vma=False,
    )
```

```python
import jax
import jax.numpy as jnp
from jax import lax
from jax.experimental import pallas as pl
from jax.experimental.pallas import tpu as pltpu
from jax.sharding import PartitionSpec as P
import functools


sigma_fractions = (1.0 / 32.0, 1.0 / 16.0, 1.0 / 8.0, 1.0 / 4.0)
kernel_weights = (1.0, 0.5, 0.25, 0.125)
force_unit = 1.0 / 4096.0
step_size = 0.5


def cosine_table(length):
    points = jnp.arange(length).astype(jnp.float32)
    angles = jnp.pi * (points[:, None] + 0.5) * points[None, :] / length
    scales = jnp.where(points == 0.0, jnp.sqrt(1.0 / length), jnp.sqrt(2.0 / length))
    return (jnp.cos(angles) * scales[None, :]).astype(jnp.bfloat16)


def occupancy(band_index, band_total):
    shifted = band_index.astype(jnp.float32) - 0.5 * band_total
    return 2.0 / (1.0 + jnp.exp(shifted / (0.125 * band_total)))


def kernels(points, centres, extent):
    values = []
    slopes = []
    for fraction in sigma_fractions:
        exponent = 0.5 / (extent * fraction) ** 2
        offset = points[:, None] - centres[None, :]
        gauss_value = jnp.exp(-exponent * offset * offset)
        values.append(gauss_value)
        slopes.append(2.0 * exponent * offset * gauss_value)
    return (jnp.concatenate(values, axis=1), jnp.concatenate(slopes, axis=1))


def peer_coords(index, sizes):
    _, gvec_size, dom_size = sizes
    return (index // (gvec_size * dom_size), (index // dom_size) % gvec_size, index % dom_size)


def gather_kernel(sizes, x_ref, out_ref, send_sem, recv_sem):
    total = sizes[0] * sizes[1] * sizes[2]
    me = (lax.axis_index("band") * sizes[1] + lax.axis_index("gvec")) * sizes[2] + lax.axis_index("dom")
    barrier = pltpu.get_barrier_semaphore()

    def greet(step, carry):
        peer = lax.rem(me + step, total)
        pl.semaphore_signal(
            barrier, inc=1, device_id=peer_coords(peer, sizes), device_id_type=pl.DeviceIdType.MESH
        )
        return carry

    def copy_of(step):
        peer = lax.rem(me + step, total)
        return pltpu.make_async_remote_copy(
            src_ref=x_ref,
            dst_ref=out_ref.at[me],
            send_sem=send_sem.at[step],
            recv_sem=recv_sem.at[step],
            device_id=peer_coords(peer, sizes),
            device_id_type=pl.DeviceIdType.MESH,
        )

    def send(step, carry):
        copy_of(step).start()
        return carry

    def finish(step, carry):
        copy_of(step).wait()
        return carry

    lax.fori_loop(1, total, greet, 0)
    out_ref[me] = x_ref[...]
    pl.semaphore_wait(barrier, total - 1)
    lax.fori_loop(1, total, send, 0)
    lax.fori_loop(1, total, finish, 0)


def gather_all(block, sizes, collective_id):
    total = sizes[0] * sizes[1] * sizes[2]
    return pl.pallas_call(
        functools.partial(gather_kernel, sizes),
        out_shape=jax.ShapeDtypeStruct((total,) + block.shape, block.dtype),
        in_specs=[pl.BlockSpec(memory_space=pltpu.VMEM)],
        out_specs=pl.BlockSpec(memory_space=pltpu.VMEM),
        scratch_shapes=[pltpu.SemaphoreType.DMA((total,)), pltpu.SemaphoreType.DMA((total,))],
        compiler_params=pltpu.CompilerParams(collective_id=collective_id, has_side_effects=True),
    )(block)


def plane_rows(x_ref, y_ref):
    rows, _ = x_ref.shape
    parts = []
    for row in range(rows):
        parts.append((x_ref[row : row + 1, :] * y_ref[...]).astype(jnp.bfloat16))
    return jnp.concatenate(parts, axis=0)


def potential_kernel(x_ref, y_ref, depth_ref, local_ref, out_ref):
    value = lax.dot_general(
        plane_rows(x_ref, y_ref),
        depth_ref[...],
        (((1,), (1,)), ((), ())),
        preferred_element_type=jnp.float32,
    )
    rounded = value.astype(jnp.bfloat16).astype(jnp.float32).reshape(out_ref.shape)
    out_ref[...] = local_ref[...].astype(jnp.float32) + rounded


def slab_potential(x_value, y_value, depth, v_local):
    x_total, y_total, z_total = v_local.shape
    width = x_value.shape[1]
    rows = 16
    return pl.pallas_call(
        potential_kernel,
        grid=(x_total // rows,),
        out_shape=jax.ShapeDtypeStruct(v_local.shape, jnp.float32),
        in_specs=[
            pl.BlockSpec((rows, width), lambda i: (i, 0)),
            pl.BlockSpec((y_total, width), lambda i: (0, 0)),
            pl.BlockSpec((z_total, width), lambda i: (0, 0)),
            pl.BlockSpec((rows, y_total, z_total), lambda i: (i, 0, 0)),
        ],
        out_specs=pl.BlockSpec((rows, y_total, z_total), lambda i: (i, 0, 0)),
        cost_estimate=pl.CostEstimate(
            flops=8 * x_total * y_total * z_total * width,
            bytes_accessed=6 * x_total * y_total * z_total,
            transcendentals=0,
        ),
        name="slab_potential",
    )(x_value, y_value, depth, v_local)


def force_kernel(xv_ref, xs_ref, yv_ref, ys_ref, real_ref, out_ref):
    @pl.when(pl.program_id(0) == 0)
    def _():
        out_ref[...] = jnp.zeros_like(out_ref)

    rows, y_total, z_total = real_ref.shape
    density = real_ref[...].astype(jnp.float32)
    density = (density * density).astype(jnp.bfloat16).reshape(rows * y_total, z_total)
    for part, (xr, yr) in enumerate(((xv_ref, yv_ref), (xs_ref, yv_ref), (xv_ref, ys_ref))):
        out_ref[part] += lax.dot_general(
            density,
            plane_rows(xr, yr),
            (((0,), (0,)), ((), ())),
            preferred_element_type=jnp.float32,
        )


def slab_moments(x_value, x_slope, y_value, y_slope, real_space):
    x_total, y_total, z_total = real_space.shape
    width = x_value.shape[1]
    rows = 16
    return pl.pallas_call(
        force_kernel,
        grid=(x_total // rows,),
        out_shape=jax.ShapeDtypeStruct((3, z_total, width), jnp.float32),
        in_specs=[
            pl.BlockSpec((rows, width), lambda i: (i, 0)),
            pl.BlockSpec((rows, width), lambda i: (i, 0)),
            pl.BlockSpec((y_total, width), lambda i: (0, 0)),
            pl.BlockSpec((y_total, width), lambda i: (0, 0)),
            pl.BlockSpec((rows, y_total, z_total), lambda i: (i, 0, 0)),
        ],
        out_specs=pl.BlockSpec((3, z_total, width), lambda i: (0, 0, 0)),
        cost_estimate=pl.CostEstimate(
            flops=12 * x_total * y_total * z_total * width,
            bytes_accessed=2 * x_total * y_total * z_total,
            transcendentals=0,
        ),
        name="slab_moments",
    )(x_value, x_slope, y_value, y_slope, real_space)


def tail_kernel(
    sizes, base, back_ref, coeff_ref, table_ref, weight_ref, head_ref,
    waves_ref, out_ref, image_ref, sums_ref, tile_ref, send_sem, recv_sem,
):
    band_size, gvec_size, dom_size = sizes
    total = band_size * gvec_size * dom_size
    band_id, gvec_id, dom_id = lax.axis_index("band"), lax.axis_index("gvec"), lax.axis_index("dom")
    me = (band_id * gvec_size + gvec_id) * dom_size + dom_id
    local_bands, x_local, extent, _ = coeff_ref.shape
    barrier = pltpu.get_barrier_semaphore()

    def peer_of(step):
        outer = step // gvec_size
        return (
            lax.rem(band_id + outer // dom_size, band_size),
            lax.rem(gvec_id + step % gvec_size, gvec_size),
            lax.rem(dom_id + outer % dom_size, dom_size),
        )

    def greet(step, carry):
        pl.semaphore_signal(
            barrier, inc=1, device_id=peer_of(step), device_id_type=pl.DeviceIdType.MESH
        )
        return carry

    lax.fori_loop(1, total, greet, 0)

    def copy_of(step):
        return pltpu.make_async_remote_copy(
            src_ref=tile_ref,
            dst_ref=out_ref.at[me],
            send_sem=send_sem.at[step],
            recv_sem=recv_sem.at[step],
            device_id=peer_of(step),
            device_id_type=pl.DeviceIdType.MESH,
        )

    def send(step, carry):
        copy_of(step).start()
        return carry

    def finish(step, carry):
        copy_of(step).wait()
        return carry

    rows = 4
    block = (rows, extent, extent)
    wave_step = jnp.pi / extent
    q_wave = lax.broadcasted_iota(jnp.int32, block[1:], 0).astype(jnp.float32) * wave_step
    l_wave = lax.broadcasted_iota(jnp.int32, block[1:], 1).astype(jnp.float32) * wave_step
    plane_kinetic = 0.5 * (q_wave * q_wave + l_wave * l_wave)

    def x_waves(index):
        first = gvec_id * x_local + index * rows
        at = lax.broadcasted_iota(jnp.int32, block, 0) + first
        return at.astype(jnp.float32) * wave_step

    def total_of(value):
        return jnp.sum(jnp.sum(value, axis=0, keepdims=True), axis=1, keepdims=True)

    spots = (
        lax.broadcasted_iota(jnp.int32, head_ref.shape, 0) * 128
        + lax.broadcasted_iota(jnp.int32, head_ref.shape, 1)
    )
    tile = head_ref[...]
    stress = [0.0] * 6
    for band in range(local_bands):
        sums_ref[...] = jnp.zeros_like(sums_ref)

        def first_pass(index, carry):
            window = pl.ds(index * rows, rows)
            wide = coeff_ref[band, window].astype(jnp.float32)
            field = jnp.dot(
                back_ref[band, window].reshape(rows * extent, extent),
                table_ref[...],
                preferred_element_type=jnp.float32,
            ).reshape(block)
            x_wave = x_waves(index)
            image = (0.5 * x_wave * x_wave + plane_kinetic[None]) * wide + field
            image_ref[band, window] = image
            square = wide * wide
            by_x = square * x_wave
            sums_ref[0] += jnp.sum(square, axis=0)
            sums_ref[1] += jnp.sum(by_x, axis=0)
            sums_ref[2] += jnp.sum(by_x * x_wave, axis=0)
            sums_ref[3] += jnp.sum(wide * image, axis=0)
            return carry

        lax.fori_loop(0, x_local // rows, first_pass, 0)
        norm = total_of(sums_ref[0])
        inner = total_of(sums_ref[3])
        filled = norm > 0.0
        energy = jnp.where(filled, inner / jnp.where(filled, norm, 1.0), 0.0)
        weight = weight_ref[0:1, band : band + 1]
        terms = (
            sums_ref[2],
            sums_ref[0] * q_wave * q_wave,
            sums_ref[0] * l_wave * l_wave,
            sums_ref[1] * q_wave,
            sums_ref[1] * l_wave,
            sums_ref[0] * q_wave * l_wave,
        )
        stress = [old + weight * total_of(term) for old, term in zip(stress, terms)]
        sums_ref[1] = jnp.zeros_like(sums_ref[1])

        def second_pass(index, carry):
            window = pl.ds(index * rows, rows)
            wide = coeff_ref[band, window].astype(jnp.float32)
            residual = image_ref[band, window] - energy[None] * wide
            sums_ref[1] += jnp.sum(residual * residual, axis=0)
            return carry

        lax.fori_loop(0, x_local // rows, second_pass, 0)
        square = total_of(sums_ref[1])
        for shift, value in enumerate((norm, inner, square)):
            tile = jnp.where(spots == base + 7 + shift * local_bands + band, value, tile)
    for shift, value in enumerate(stress):
        tile = jnp.where(spots == base + shift, value / float(extent**3), tile)
    tile_ref[...] = tile
    out_ref[me] = tile
    pl.semaphore_wait(barrier, total - 1)
    lax.fori_loop(1, total, send, 0)
    lax.fori_loop(1, gvec_size, finish, 0)

    both = tile
    for step in range(1, gvec_size):
        other = lax.rem(gvec_id + step, gvec_size)
        both = both + out_ref[(band_id * gvec_size + other) * dom_size + dom_id]
    for band in range(local_bands):
        norm = total_of(jnp.where(spots == base + 7 + band, both, 0.0))
        inner = total_of(jnp.where(spots == base + 7 + local_bands + band, both, 0.0))
        energy = inner / norm

        def last_pass(index, carry):
            window = pl.ds(index * rows, rows)
            wide = coeff_ref[band, window].astype(jnp.float32)
            x_wave = x_waves(index)
            kinetic = 0.5 * x_wave * x_wave + plane_kinetic[None]
            residual = image_ref[band, window] - energy[None] * wide
            updated = wide - step_size * residual / (1.0 + kinetic)
            waves_ref[band, window] = updated.astype(jnp.bfloat16)
            return carry

        lax.fori_loop(0, x_local // rows, last_pass, 0)
    lax.fori_loop(gvec_size, total, finish, 0)


def tail(back_two, coeffs, cosines, weight, head, base, sizes):
    total = sizes[0] * sizes[1] * sizes[2]
    extent = coeffs.shape[-1]
    vmem = pl.BlockSpec(memory_space=pltpu.VMEM)
    return pl.pallas_call(
        functools.partial(tail_kernel, sizes, base),
        out_shape=(
            jax.ShapeDtypeStruct(coeffs.shape, jnp.bfloat16),
            jax.ShapeDtypeStruct((total,) + head.shape, jnp.float32),
        ),
        in_specs=[vmem] * 5,
        out_specs=(vmem, vmem),
        scratch_shapes=[
            pltpu.VMEM(coeffs.shape, jnp.float32),
            pltpu.VMEM((4, extent, extent), jnp.float32),
            pltpu.VMEM(head.shape, jnp.float32),
            pltpu.SemaphoreType.DMA((total,)),
            pltpu.SemaphoreType.DMA((total,)),
        ],
        compiler_params=pltpu.CompilerParams(
            collective_id=1, has_side_effects=True, vmem_limit_bytes=40 * 1024 * 1024
        ),
        name="tail",
    )(back_two, coeffs, cosines, weight, head)


def step_body(sizes, *arrays):
    return per_device(sizes, *arrays)


def per_device(sizes, coeffs, v_local, atom_pos, atom_charge, near_list, live_count):
    local_bands, x_local, extent, _ = coeffs.shape
    cosines = cosine_table(extent)
    gvec_id = lax.axis_index("gvec")
    group_id = lax.axis_index("band") * sizes[2] + lax.axis_index("dom")
    me = (lax.axis_index("band") * sizes[1] + gvec_id) * sizes[2] + lax.axis_index("dom")
    groups = sizes[0] * sizes[2]
    devices = groups * sizes[1]
    band_total = local_bands * groups
    cell_count = float(extent**3)
    band_ids = group_id * local_bands + jnp.arange(local_bands)
    weight = occupancy(band_ids, band_total)
    capacity = near_list.shape[0]
    live_mask = (jnp.arange(capacity) < live_count[0]).astype(jnp.float32)
    picked_pos = jnp.take(atom_pos, near_list, axis=1)
    picked_charge = jnp.take(atom_charge, near_list) * live_mask
    own_block = jnp.concatenate([picked_pos, picked_charge[None, :], live_mask[None, :]], axis=0)
    lanes = -(-capacity // 128) * 128
    tile = jnp.pad(own_block, ((0, 3), (0, lanes - capacity)))
    gathered = gather_all(tile, sizes, 0)
    coeffs, gathered = lax.optimization_barrier((coeffs, gathered))
    all_blocks = gathered[:, :5, :capacity].transpose(1, 0, 2).reshape(5, devices * capacity)
    live_total = all_blocks.shape[1] // 4
    order = jnp.cumsum(all_blocks[4]) - 1.0
    target = jnp.where(all_blocks[4] > 0.5, order, float(live_total)).astype(jnp.int32)
    select = (target[:, None] == jnp.arange(live_total)[None, :]).astype(jnp.float32)
    charges = jnp.dot(all_blocks[:4], select, precision=lax.Precision.HIGHEST)

    y_share = v_local.shape[1]
    x_points = jnp.arange(extent).astype(jnp.float32)
    y_points = (gvec_id * y_share + jnp.arange(y_share)).astype(jnp.float32)
    x_value, x_slope = kernels(x_points, charges[0], extent)
    y_value, y_slope = kernels(y_points, charges[1], extent)
    z_value, z_slope = kernels(x_points, charges[2], extent)
    weights = jnp.array(kernel_weights, jnp.float32)
    scaled = (weights[:, None] * charges[3][None, :]).reshape(-1)
    depth = (scaled[None, :] * z_value).astype(jnp.bfloat16)

    gvec_size = sizes[1]
    chunks = 2 if y_share % 32 == 0 else 1
    chunk = y_share // chunks

    def y_rows(step, part):
        owner = lax.rem(gvec_id + step + gvec_size, gvec_size)
        return lax.dynamic_slice_in_dim(cosines, owner * y_share + part * chunk, chunk, 0)

    def a_columns(step):
        owner = lax.rem(gvec_id + step, gvec_size)
        return lax.dynamic_slice_in_dim(cosines, owner * x_local, x_local, 1)

    def shift(value, step):
        return lax.ppermute(
            value, "gvec", [(at, (at + step) % gvec_size) for at in range(gvec_size)]
        )

    section_z = jnp.einsum(
        "naql,zl->naqz", coeffs, cosines, preferred_element_type=jnp.float32
    ).astype(jnp.bfloat16)

    def section_y(step, part):
        return jnp.einsum(
            "naqz,yq->nayz", section_z, y_rows(step, part), preferred_element_type=jnp.float32
        ).astype(jnp.bfloat16)

    arrived = []
    for part in range(chunks):
        leaving = [section_y(-step, part) for step in range(1, gvec_size)]
        if part > 0:
            leaving, arrived[-1], depth = lax.optimization_barrier((leaving, arrived[-1], depth))
        arrived.append([shift(block, -step) for step, block in enumerate(leaving, 1)])
    field_total = slab_potential(x_value, y_value, depth, v_local)
    moments = 0.0
    reals = []
    returned = []
    own_sections = [section_y(0, part) for part in range(chunks)]
    for part in range(chunks):
        window = slice(part * chunk, (part + 1) * chunk)
        held = [own_sections[part]] + arrived[part]
        real_space = sum(
            jnp.einsum("nayz,xa->nxyz", block, a_columns(step), preferred_element_type=jnp.float32)
            for step, block in enumerate(held)
        ).astype(jnp.bfloat16)
        applied = (field_total[None, :, window] * real_space.astype(jnp.float32)).astype(jnp.bfloat16)

        def back_x(step):
            return jnp.einsum(
                "nxyz,xa->nayz", applied, a_columns(step), preferred_element_type=jnp.float32
            ).astype(jnp.bfloat16)

        sent = [back_x(step) for step in range(1, gvec_size)]
        if part == chunks - 1:
            sent, reals = lax.optimization_barrier((sent, reals + [real_space]))
        else:
            reals.append(real_space)
            sent, arrived[part + 1] = lax.optimization_barrier((sent, arrived[part + 1]))
        moved = [shift(block, step) for step, block in enumerate(sent, 1)]
        returned.append(moved + [back_x(0)])
    for part in range(chunks):
        window = slice(part * chunk, (part + 1) * chunk)
        for band in range(local_bands):
            moments = moments + weight[band] * slab_moments(
                x_value, x_slope, y_value[window], y_slope[window], reals[part][band]
            )
    embedding = jnp.sum(moments[0] * depth.astype(jnp.float32)) / cell_count
    force_terms = jnp.stack(
        [
            jnp.sum(moments[1] * z_value, axis=0),
            jnp.sum(moments[2] * z_value, axis=0),
            jnp.sum(moments[0] * z_slope, axis=0),
        ]
    )
    force_terms = force_terms * scaled[None, :]
    forces = -force_unit * jnp.sum(force_terms.reshape(3, len(kernel_weights), -1), axis=1)

    steps = list(range(-1, -gvec_size, -1)) + [0]
    back_two = sum(
        jnp.einsum("nayz,yq->naqz", block, y_rows(step, part), preferred_element_type=jnp.float32)
        for part in range(chunks)
        for step, block in zip(steps, returned[part])
    ).astype(jnp.bfloat16)
    mine = (jnp.arange(band_total)[None, :] == band_ids[:, None]).astype(jnp.float32)
    flat = jnp.concatenate([forces.reshape(-1), jnp.zeros((6,), jnp.float32), embedding[None]])
    tail_length = flat.shape[0] + 3 * local_bands
    flat = jnp.pad(flat, (0, 3 * local_bands + -tail_length % 1024)).reshape(-1, 128)
    weight_row = jnp.pad(weight, (0, -local_bands % 128))[None, :]
    waves_new, parts = tail(back_two, coeffs, cosines, weight_row, flat, 3 * live_total, sizes)
    parts = parts.reshape(devices, -1)
    lines = 3 * live_total + 7
    summed = jnp.sum(parts[:, :lines], axis=0)
    force_all = summed[: 3 * live_total].reshape(3, live_total)
    by_group = parts[:, lines : lines + 3 * local_bands].reshape(
        sizes[0], gvec_size, sizes[2], 3, local_bands
    )
    norms, inners, squares = by_group[:, :, :, 0], by_group[:, :, :, 1], by_group[:, :, :, 2]
    norm_all = jnp.sum(norms, axis=1)
    energy_all = jnp.sum(inners, axis=1) / norm_all
    own_all = jnp.where(norms > 0.0, inners / jnp.where(norms > 0.0, norms, 1.0), 0.0)
    shifted = energy_all[:, None] - own_all
    ratio_all = (jnp.sum(squares + shifted * shifted * norms, axis=1) / norm_all).reshape(-1)
    energy_all = energy_all.reshape(-1)
    energies = jnp.sum(mine * energy_all[None, :], axis=1)
    resid_ratio = jnp.sum(mine * ratio_all[None, :], axis=1)
    band_energy = jnp.sum(occupancy(jnp.arange(band_total), band_total) * energy_all) / band_total
    totals = jnp.concatenate([summed[3 * live_total : 3 * live_total + 7], band_energy[None]])
    start = lax.dynamic_slice(order, (me * capacity,), (capacity,))
    own_target = jnp.where(live_mask > 0.5, start, float(live_total)).astype(jnp.int32)
    slot_select = (own_target[None, :] == jnp.arange(live_total)[:, None]).astype(jnp.float32)
    slot_force = jnp.dot(force_all, slot_select, precision=lax.Precision.HIGHEST)
    atom_select = (near_list[:, None] == jnp.arange(atom_pos.shape[1])[None, :]).astype(jnp.float32)
    atom_force = jnp.dot(slot_force, atom_select, precision=lax.Precision.HIGHEST)
    return (waves_new, energies, resid_ratio, atom_force, totals)


def solution(mesh):
    sizes = (mesh.shape["band"], mesh.shape["gvec"], mesh.shape["dom"])
    return jax.shard_map(
        functools.partial(step_body, sizes),
        mesh=mesh,
        in_specs=(
            P(("band", "dom"), "gvec", None, None),
            P(None, "gvec", None),
            P(None, ("band", "gvec", "dom")),
            P(("band", "gvec", "dom")),
            P(("band", "gvec", "dom")),
            P(("band", "gvec", "dom")),
        ),
        out_specs=(
            P(("band", "dom"), "gvec", None, None),
            P(("band", "dom")),
            P(("band", "dom")),
            P(None, ("band", "gvec", "dom")),
            P(),
        ),
        check_vma=False,
    )
```
